256 devices in a mesh: gx: 16 (over y_lo, z), gy: 16 (over y_hi, x, core).
Axes of the slice: x: 4, y: 4 (y_hi: 2, y_lo: 2; y = y_hi * 2 + y_lo), z: 8, core: 2. Of those that a mesh axis runs over, the one named last changes fastest.
Arguments:
- tokens: bfloat16 [8192, 2048], P('gx', 'gy'), may hold values from -40 to 40
- norm_gain: float32 [2048], replicated, may hold values from 0.25 to 1.75
- expert_ids: int32 [8192, 6], P('gx'), may hold values from 0 to 63, all different within a row; in each aligned block of 512 rows (0 to 511, 512 to 1023, ...) at most 64 rows name the same one
- gate_weights: float32 [8192, 6], P('gx'), may hold values from 0.05 to 0.35
- shared_in: bfloat16 [2, 2048, 2816], P(None, 'gx', 'gy'), may hold values from -0.125 to 0.125
- shared_out: bfloat16 [2816, 2048], P('gy', 'gx'), may hold values from -0.109375 to 0.109375
- expert_in: bfloat16 [256, 2048, 704], P(('gx', 'gy')), may hold values from -0.125 to 0.125
- expert_out: bfloat16 [256, 352, 2048], P(('gx', 'gy')), may hold values from -0.15625 to 0.15625
Outputs:
- combined: bfloat16 [8192, 2048], P('gx', 'gy')
The draws below stay inside these ranges and needn't reach their ends.
Inputs may be any that keep to these rules, and one draw needn't show every extreme that they name: `expert_ids`: each row names 6 different experts. In each aligned block of 512 rows (the tokens of one index of gx) no expert is named by more than 64 rows, and in some block one expert is named by exactly 64.
All inputs are finite; a program needn't handle non-finite values.
Results may differ from the reference program's by a relative error of at most 0.017.
Values may be sent and summed in bfloat16 or wider, within the bound.
A program may use at most 64 MiB of HBM per device.

```python
import math
import jax
import jax.numpy as jnp
import numpy as np
from jax import lax

D = 2048
FF = 1408
EXPERTS = 64
TOPK = 6
SFF = 2816
TOK_DEV = 512
TOKENS = 8192
CAP = 64
FF_SPLIT = 4
FF_PART = 352
HELD = 1
N_GX = 16
N_GY = 16


def draw_tokens(key, part):
    first, second, third = jax.random.split(key, 3)
    column_scale = jnp.exp(jax.random.uniform(first, (1, D), jnp.float32, 0.0, math.log(10.0)))
    row_scale = jnp.exp(jax.random.uniform(second, (TOKENS, 1), jnp.float32, 0.0, math.log(10.0)))
    base = jax.random.truncated_normal(third, -4.0, 4.0, (TOKENS, D), jnp.float32)
    return (base * row_scale * column_scale * 0.1).astype(jnp.bfloat16)


def block_scale(key, shape, pieces, smallest, top_value):
    gain, own = 1.0, jax.random.fold_in(key, 6)
    for position, blocks in pieces:
        steps = jnp.exp(jax.random.uniform(jax.random.fold_in(own, position), (blocks,), jnp.float32, smallest / len(pieces), top_value / len(pieces)))
        gain = gain * jnp.repeat(steps, shape[position] // blocks).reshape([-1 if axis == position else 1 for axis in range(len(shape))])
    return gain


def routed_block(own_key, own, number, rows, count, top, bound, skew):
    sequence = jax.random.permutation(own_key, count)
    crowded, ordinary = load_shares(count, rows * top, bound, skew, True), load_shares(count, rows * top, bound, skew, False)
    places = jnp.arange(count)

    def named(lengths, offset_by):
        used = int((lengths > 0).sum())
        fixed = max(1, used // 4)
        shifted = fixed + (places - fixed + offset_by * (used - fixed)) % max(1, count - fixed)
        return jnp.zeros((count,), jnp.int32).at[sequence[jnp.where(places < fixed, places, shifted)]].set(jnp.asarray(lengths, jnp.int32))

    lengths = jnp.where(number % 4 == 0, named(crowded, number // 4), named(ordinary, number - number // 4 - 1))
    mixed = jax.random.permutation(jax.random.fold_in(own, 3), count)
    donor, receiver = mixed[0:count // 2 * 2:2], mixed[1:count // 2 * 2:2]
    margin = jnp.minimum(lengths[donor] - 1, bound - lengths[receiver]) // 2
    margin = jnp.where((donor == sequence[0]) | (receiver == sequence[0]) | (lengths[receiver] == 0), 0, jnp.maximum(margin, 0))
    shifted = jax.random.randint(jax.random.fold_in(own, 4), (count // 2,), 0, 1 << 20) % (margin + 1)
    lengths = lengths.at[donor].add(-shifted).at[receiver].add(shifted)
    members = jnp.searchsorted(jnp.cumsum(lengths), jnp.arange(rows * top), side="right").astype(jnp.int32)
    grid = members.reshape(top, rows).T
    grid = grid[jax.random.permutation(jax.random.fold_in(own, 1), rows)]
    offset_by = jax.random.randint(jax.random.fold_in(own, 2), (rows, 1), 0, top)
    return jnp.take_along_axis(grid, (jnp.arange(top)[None, :] + offset_by) % top, axis=1)


def load_shares(amount, total, bound, lean, full):
    portions = [(1 << 20) // math.isqrt(rank ** lean) + 1 for rank in range(1, amount + 1)]
    largest = bound if full else min(bound, max(-(-total // amount), total * portions[0] // sum(portions)))
    least = 1 if total - largest >= amount - 1 else 0
    holding, spare = [largest] + [least] * (amount - 1), total - largest - least * (amount - 1)
    while spare > 0:
        free = [i for i in range(1, amount) if holding[i] < largest] or [i for i in range(1, amount) if holding[i] < bound]
        pool, budget = sum([portions[i] for i in free]), spare
        for i in free:
            addition = min(bound - holding[i], max(1, budget * portions[i] // pool), spare)
            holding[i] = holding[i] + addition
            spare = spare - addition
    return np.array(holding)


def scatter_about(key, extent, spread, reach, cuts=(), kind=jnp.bfloat16):
    level = block_scale(key, extent, cuts, -0.22, 0.18) if cuts else 1.0
    entries = jax.random.normal(key, extent, jnp.float32) * spread * level
    return jnp.minimum(jnp.maximum(entries, -reach), reach).astype(kind)


def setup_inputs(seed: int = 0) -> dict:
    splits = jax.random.split(jax.random.key(seed), 9)
    tokens = draw_tokens(jax.random.fold_in(splits[8], 71), 0)
    norm_gain = jnp.clip(1.0 + 0.15 * jax.random.normal(splits[1], (D,), jnp.float32), 0.25, 1.75)
    expert_ids_keys = jax.random.split(jax.random.fold_in(splits[2], 1), TOKENS // TOK_DEV)
    expert_ids_turns = jax.random.permutation(jax.random.fold_in(splits[2], 3), TOKENS // TOK_DEV)
    expert_ids = jax.vmap(lambda own, number: routed_block(jax.random.fold_in(splits[2], 2), own, number, TOK_DEV, EXPERTS, TOPK, CAP, 2))(expert_ids_keys, expert_ids_turns).reshape((TOKENS, TOPK))
    gate_weights = jnp.clip(0.05 + 0.29999999 * jax.random.uniform(splits[3], (TOKENS, TOPK), jnp.float32) ** block_scale(splits[3], (TOKENS, TOPK), ((0, 16),), -0.2, 0.2), 0.05, 0.35)
    shared_in = scatter_about(splits[4], (2, D, SFF), D ** -0.5, 0.125, ((1, 16), (2, 16)))
    shared_out = scatter_about(splits[5], (SFF, D), SFF ** -0.5, 0.109375, ((0, 16), (1, 16)))
    expert_in = scatter_about(splits[6], (EXPERTS * FF_SPLIT, D, 2 * FF_PART), D ** -0.5, 0.125, ((0, 256),))
    expert_out = scatter_about(splits[7], (EXPERTS * FF_SPLIT, FF_PART, D), FF ** -0.5, 0.15625, ((0, 256),))
    return {"tokens": tokens, "norm_gain": norm_gain, "expert_ids": expert_ids, "gate_weights": gate_weights, "shared_in": shared_in, "shared_out": shared_out, "expert_in": expert_in, "expert_out": expert_out}


epsilon = 1e-06

def reference(tokens, norm_gain, expert_ids, gate_weights, shared_in, shared_out, expert_in, expert_out):
    values = tokens.astype(jnp.float32)
    inverse_rms = lax.rsqrt(lax.optimization_barrier(jnp.mean(values * values, axis=1, keepdims=True)) + epsilon)
    normed = (values * inverse_rms * norm_gain).astype(jnp.bfloat16)
    shared_gate = jnp.dot(normed, shared_in[0], preferred_element_type=jnp.float32)
    shared_up = jnp.dot(normed, shared_in[1], preferred_element_type=jnp.float32)
    shared_hidden = (jax.nn.silu(shared_gate) * shared_up).astype(jnp.bfloat16)
    group_units = SFF // N_GY
    hidden_groups = shared_hidden.reshape(TOKENS, N_GY, group_units).astype(jnp.float32)
    out_groups = shared_out.reshape(N_GY, group_units, D).astype(jnp.float32)
    start_sums = jnp.einsum('tgf,gfd->gtd', hidden_groups, out_groups)
    block_routes = expert_ids.reshape(N_GX, TOK_DEV * TOPK)
    one_hot = (block_routes[:, :, None] == jnp.arange(EXPERTS, dtype=jnp.int32)[None, None, :]).astype(jnp.int32)
    earlier_count = (jnp.cumsum(one_hot, axis=1).astype(jnp.int32) - one_hot).astype(jnp.int32)
    slot_index = lax.optimization_barrier(jnp.sum(earlier_count * one_hot, axis=2)).astype(jnp.int32)
    block_base = (jnp.arange(N_GX, dtype=jnp.int32) * CAP)[:, None]
    slot_place = (block_base + slot_index).astype(jnp.int32).reshape(TOKENS, TOPK)
    token_index = jnp.arange(TOKENS, dtype=jnp.int32)
    buffer_rows = N_GX * CAP
    experts_in = expert_in.reshape(EXPERTS, FF_SPLIT, D, 2 * FF_PART)
    experts_out = expert_out.reshape(EXPERTS, FF_SPLIT, FF_PART, D)
    padded = jnp.concatenate([normed, jnp.zeros((1, D), jnp.bfloat16)], axis=0)

    def one_expert(running, expert):
        chosen = expert_ids == expert
        weight = lax.optimization_barrier(jnp.sum(jnp.where(chosen, gate_weights, jnp.float32(0.0)), axis=1))
        place_here = lax.optimization_barrier(jnp.sum(jnp.where(chosen, slot_place, 0), axis=1)).astype(jnp.int32)
        routed_here = jnp.any(chosen, axis=1)
        target = jnp.where(routed_here, place_here, buffer_rows).astype(jnp.int32)
        source = jnp.full((buffer_rows + 1,), TOKENS, jnp.int32).at[target].set(token_index)[:buffer_rows]
        slot_rows = padded[source]
        weights_in = lax.dynamic_index_in_dim(experts_in, expert, 0, keepdims=False)
        weights_out = lax.dynamic_index_in_dim(experts_out, expert, 0, keepdims=False)
        for slice_number in range(FF_SPLIT):
            gate_up = jnp.dot(slot_rows, weights_in[slice_number], preferred_element_type=jnp.float32)
            hidden = (jax.nn.silu(gate_up[:, :FF_PART]) * gate_up[:, FF_PART:]).astype(jnp.bfloat16)
            piece = jnp.dot(hidden, weights_out[slice_number], preferred_element_type=jnp.float32).astype(jnp.bfloat16)
            piece = lax.optimization_barrier(piece)
            contribution = weight[:, None] * piece.astype(jnp.float32)[place_here]
            group = ((expert * FF_SPLIT + slice_number) // HELD % N_GY).astype(jnp.int32)
            running = running.at[group].add(contribution)
        return (running, None)
    totals, _ = lax.scan(one_expert, start_sums, jnp.arange(EXPERTS, dtype=jnp.int32))
    group_partial = lax.optimization_barrier(totals.astype(jnp.bfloat16))
    return lax.optimization_barrier(jnp.sum(group_partial.astype(jnp.float32), axis=0)).astype(jnp.bfloat16)
```

```python
import jax
import jax.numpy as jnp
from jax import lax
from jax.experimental import pallas as pl
from jax.experimental.pallas import tpu as pltpu
from jax.sharding import PartitionSpec as P

MESH = pl.DeviceIdType.MESH
F32 = jnp.float32
BF16 = jnp.bfloat16
EPSILON = 1e-06

NX = 16
NY = 16
CAP = 64
TOK = 512
D = 2048
B = 128
Q = 512
TOPK = 6
PART = 352
SPART = 176
CH = 256
VMEM_LIMIT = 60 * 1024 * 1024


def kernel(
    tok, gain, idst, gatet, shin, shout, win_hbm, wout_hbm, out,
    xall, win, wout, wsin, wsout, code, gm, oh, og, snd, rx, xn, sa, sibin, po, pn, sn, nbrin, ret, back,
    acc, fs, fin, ssa, ssin, spo, spn, sb, shr,
    ld_sem, tok_s, tok_r, tf_s, tf_r, wz_s, wz_r, wy_s, wy_r, dp_s, dp_r, nb_s, nb_r, sq_s, sq_r,
    ra_s, ra_r, rb_s, rb_r, bk_s, bk_r, xs_s, xs_r, sr_s, sr_r, fn_s, fn_r,
):
    gx = lax.axis_index("gx")
    gy = lax.axis_index("gy")
    j, q = gy // 4, gy % 4
    ylo, z = gx // 8, gx % 8
    sib = gy + 1 - 2 * (gy % 2)
    nbr = gy + 2 - 4 * ((gy // 2) % 2)
    qs, qn = sib % 4, nbr % 4
    qsn = (qs + 2) % 4
    ypart = (gx + 8) % NX

    def peer(r):
        return (gy + r) % NY

    def remote(src, dst, send, recv, tx, ty):
        return pltpu.make_async_remote_copy(
            src_ref=src, dst_ref=dst, send_sem=send, recv_sem=recv,
            device_id=(tx, ty), device_id_type=MESH,
        )

    def shift(k, u):
        return 4 * u + (k + 3) % 4

    def loads():
        for i in range(16):
            p = (i % 4) * 4 + i // 4
            yield pltpu.make_async_copy(
                win_hbm.at[pl.ds(i * B, B), :], win.at[pl.ds(p * B, B), :], ld_sem.at[0, i]
            )
            yield pltpu.make_async_copy(
                wout_hbm.at[:, pl.ds(i * B, B)], wout.at[i % 4, :, pl.ds((i // 4) * B, B)], ld_sem.at[1, i]
            )

    for copy in loads():
        copy.start()

    barrier = pltpu.get_barrier_semaphore()
    for r in range(1, NX):
        pl.semaphore_signal(barrier, inc=1, device_id=((gx + r) % NX, gy), device_id_type=MESH)
    for r in range(1, 8):
        pl.semaphore_signal(barrier, inc=1, device_id=(gx, peer(2 * r)), device_id_type=MESH)
    pl.semaphore_signal(barrier, inc=1, device_id=(gx, sib), device_id_type=MESH)
    pl.semaphore_wait(barrier, NX - 1 + 8)

    def tok_at(owner):
        return xall.at[owner % 4, :, pl.ds(pl.multiple_of((owner // 4) * B, B), B)]

    def tok_send(r):
        return remote(tok, tok_at(gy), tok_s.at[r], tok_r.at[r], gx, peer(2 * r))

    def tok_recv(r):
        place = tok_at(peer(16 - 2 * r))
        return remote(place, place, tok_s.at[r], tok_r.at[r], gx, sib)

    def tok_forward(r):
        place = tok_at(peer(16 - 2 * r))
        return remote(place, place, tf_s.at[r], tf_r.at[r], gx, sib)

    def tok_forwarded(r):
        place = tok_at((sib + 16 - 2 * r) % NY)
        return remote(place, place, tf_s.at[r], tf_r.at[r], gx, sib)

    tok_own = remote(tok, tok_at(gy), tf_s.at[0], tf_r.at[0], gx, sib)
    for r in (2, 4, 6):
        tok_send(r).start()

    def block_z(e):
        if e == 0:
            return z
        step = (e + 1) // 2
        return (z + 8 - step) % 8 if e % 2 else (z + step) % 8

    def w_at(owner):
        place = (owner % 4) * 4 + owner // 4
        return (
            wsin.at[:, pl.ds(pl.multiple_of(place * B, B), B), :],
            wsout.at[owner % 4, :, pl.ds(pl.multiple_of((owner // 4) * B, B), B)],
        )

    def w_source(e):
        return (shin, shout) if e == 0 else w_at(ylo * 8 + block_z(e))

    def w_ring(e):
        origin = 0 if e <= 2 else e - 2
        target = ylo * 8 + ((z + 1) % 8 if e % 2 else (z + 7) % 8)
        to = w_at(ylo * 8 + block_z(origin))
        return [
            remote(w_source(origin)[t], to[t], wz_s.at[t, e], wz_r.at[t, e], target, gy) for t in range(2)
        ]

    def w_ring_recv(e):
        place = w_at(ylo * 8 + block_z(e))
        return [remote(place[t], place[t], wz_s.at[t, e], wz_r.at[t, e], ypart, gy) for t in range(2)]

    def w_cross(e):
        to = w_at(ylo * 8 + block_z(e))
        return [remote(w_source(e)[t], to[t], wy_s.at[t, e], wy_r.at[t, e], ypart, gy) for t in range(2)]

    def w_cross_recv(e):
        place = w_at((1 - ylo) * 8 + block_z(e))
        return [remote(place[t], place[t], wy_s.at[t, e], wy_r.at[t, e], ypart, gy) for t in range(2)]

    def start(copies):
        for copy in copies:
            copy.start()

    def arrived(copies):
        for copy in copies:
            copy.wait_recv()

    start(w_ring(1))
    start(w_ring(2))
    tok_own.start()
    for r in (1, 3, 5, 7):
        tok_send(r).start()
    start(w_cross(0))

    xall[q, :, pl.ds(pl.multiple_of(j * B, B), B)] = tok[...]
    wsin[:, pl.ds(pl.multiple_of(((gx % 4) * 4 + gx // 4) * B, B), B), :] = shin[...]
    wsout[gx % 4, :, pl.ds(pl.multiple_of((gx // 4) * B, B), B)] = shout[...]

    expert = 4 * lax.broadcasted_iota(jnp.int32, (NX, TOK), 0) + j
    named = jnp.zeros((NX, TOK), F32)
    weight = jnp.zeros((NX, TOK), F32)
    for k in range(TOPK):
        hit = idst[k : k + 1, :] == expert
        named = jnp.where(hit, 1.0, named)
        weight = jnp.where(hit, gatet[k : k + 1, :], weight)
    before = (
        lax.broadcasted_iota(jnp.int32, (TOK, TOK), 0) < lax.broadcasted_iota(jnp.int32, (TOK, TOK), 1)
    )
    count = jnp.dot(
        named.astype(BF16), jnp.where(before, 1.0, 0.0).astype(BF16), preferred_element_type=F32
    )
    code[...] = jnp.where(named > 0.0, count, -1.0)
    gm[...] = weight
    slot = lax.broadcasted_iota(jnp.int32, (CAP, TOK), 0).astype(F32)

    def build(k, carry):
        for u in range(4):
            m = (gx + shift(k, u)) % NX
            hit = slot == code[pl.ds(m, 1), :]
            at = pl.multiple_of((4 * k + u) * CAP, CAP)
            oh[pl.ds(at, CAP), :] = jnp.where(hit, 1.0, 0.0).astype(BF16)
            og[pl.ds(at, CAP), :] = jnp.where(hit, gm[pl.ds(m, 1), :], 0.0).astype(BF16)
        return carry

    lax.fori_loop(0, 4, build, 0)

    def slots_of(k, u):
        return pl.ds(pl.multiple_of((4 * k + u) * CAP, CAP), CAP)

    def chunk_of(k):
        return pl.ds(pl.multiple_of(k * CH, CH), CH)

    def dp(k, u):
        return remote(
            snd.at[slots_of(k, u), :], rx.at[q, slots_of(k, u), :],
            dp_s.at[4 * k + u], dp_r.at[4 * k + u], (gx + shift(k, u)) % NX, gy,
        )

    def when_self(k, u, own, other):
        if u == 0:
            pl.when(k == 1)(own)
            pl.when(k != 1)(other)
        else:
            other()

    for r in (2, 4, 6):
        tok_recv(r).wait_recv()

    def dispatch(k, carry):
        picked = jnp.dot(oh[chunk_of(k), :], xall[q], preferred_element_type=F32)
        snd[chunk_of(k), :] = picked.astype(BF16)
        for u in range(4):
            def own(u=u):
                pltpu.make_async_copy(
                    snd.at[slots_of(k, u), :], rx.at[q, slots_of(k, u), :], dp_r.at[4 * k + u]
                ).start()

            when_self(k, u, own, lambda u=u: dp(k, u).start())
        return carry

    lax.fori_loop(0, 4, dispatch, 0)

    for e in (1, 2):
        arrived(w_ring_recv(e))
        start(w_ring(e + 2))
        start(w_cross(e))
    for r in (2, 4, 6):
        tok_forward(r).start()
    for r in (1, 3, 5, 7):
        tok_recv(r).wait_recv()
        tok_forward(r).start()
    for e in (3, 4):
        arrived(w_ring_recv(e))
        start(w_ring(e + 2))
        start(w_cross(e))

    def to_nbr(k):
        place = rx.at[q, chunk_of(k), :]
        return remote(place, place, nb_s.at[k], nb_r.at[k], gx, nbr)

    def from_nbr(k):
        place = rx.at[qn, chunk_of(k), :]
        return remote(place, place, nb_s.at[k], nb_r.at[k], gx, nbr)

    def to_sib(t, k):
        place = rx.at[q if t == 0 else qn, chunk_of(k), :]
        return remote(place, place, sq_s.at[t, k], sq_r.at[t, k], gx, sib)

    def from_sib(t, k):
        place = rx.at[qs if t == 0 else qsn, chunk_of(k), :]
        return remote(place, place, sq_s.at[t, k], sq_r.at[t, k], gx, sib)

    def stage_a(k):
        for u in range(4):
            place = rx.at[q, slots_of(k, u), :]
            remote(place, place, dp_s.at[4 * k + u], dp_r.at[4 * k + u], gx, sib).wait_recv()
        to_nbr(k).start()
        to_sib(0, k).start()

    def stage_a2(k):
        from_nbr(k).wait_recv()
        to_sib(1, k).start()

    def ra(k):
        return remote(sa.at[k], sibin.at[k], ra_s.at[k], ra_r.at[k], gx, sib)

    def rb(k):
        return remote(sn.at[k], nbrin.at[k], rb_s.at[k], rb_r.at[k], gx, nbr)

    def bk(k, u):
        return remote(
            ret.at[slots_of(k, u), :], back.at[slots_of(k, u), :],
            bk_s.at[4 * k + u], bk_r.at[4 * k + u], (gx + NX - shift(k, u)) % NX, gy,
        )

    def normalise(source, rows):
        total = jnp.zeros((CH, B), F32)
        for c in range(4):
            for b in range(4):
                value = source[c, rows, b * B : (b + 1) * B].astype(F32)
                total = total + value * value
        inverse = lax.rsqrt(jnp.sum(total, axis=1, keepdims=True) * (1.0 / D) + EPSILON)
        for c in range(4):
            value = source[c, rows, :].astype(F32)
            xn[:, c * Q : (c + 1) * Q] = (value * inverse * gain[c]).astype(BF16)

    def stage_b(k):
        from_sib(0, k).wait_recv()
        from_sib(1, k).wait_recv()
        normalise(rx, chunk_of(k))
        gate_up = jnp.dot(xn[...], win[...], preferred_element_type=F32)
        hidden = (jax.nn.silu(gate_up[:, :PART]) * gate_up[:, PART:]).astype(BF16)
        sa[k, 0] = jnp.dot(hidden, wout[qs], preferred_element_type=F32).astype(BF16)
        sa[k, 1] = jnp.dot(hidden, wout[qsn], preferred_element_type=F32).astype(BF16)
        ra(k).start()
        pn[k % 2] = jnp.dot(hidden, wout[qn], preferred_element_type=F32)
        po[k % 2] = jnp.dot(hidden, wout[q], preferred_element_type=F32)

    def stage_rb(k):
        remote(sa.at[k], sibin.at[k], ra_s.at[k], ra_r.at[k], gx, sib).wait_recv()
        sn[k] = (pn[k % 2] + sibin[k, 1].astype(F32)).astype(BF16)
        rb(k).start()
        po[k % 2] = po[k % 2] + sibin[k, 0].astype(F32)

    def stage_c(k):
        remote(sn.at[k], nbrin.at[k], rb_s.at[k], rb_r.at[k], gx, nbr).wait_recv()
        ret[chunk_of(k), :] = (po[k % 2] + nbrin[k].astype(F32)).astype(BF16)
        for u in range(4):
            def own(u=u):
                pltpu.make_async_copy(
                    ret.at[slots_of(k, u), :], back.at[slots_of(k, u), :], bk_r.at[4 * k + u]
                ).start()

            when_self(k, u, own, lambda u=u: bk(k, u).start())

    stage_a(0)
    for e in (5, 6):
        arrived(w_ring_recv(e))
        if e == 5:
            start(w_ring(7))
        start(w_cross(e))
    for copy in loads():
        copy.wait()

    def routed(it, carry):
        @pl.when(it < 3)
        def _():
            stage_a(it + 1)

        @pl.when(it < 4)
        def _():
            stage_a2(it)

        @pl.when(it > 0)
        def _():
            stage_rb(it - 1)

        @pl.when(it < 4)
        def _():
            stage_b(it)

        @pl.when(it > 0)
        def _():
            stage_c(it - 1)

        return carry

    lax.fori_loop(0, 5, routed, 0)

    arrived(w_ring_recv(7))
    start(w_cross(7))
    tok_forwarded(0).wait_recv()
    for r in range(1, 8):
        tok_forwarded(r).wait_recv()
    for e in range(8):
        arrived(w_cross_recv(e))

    def shared(c, carry):
        rows = chunk_of(c)
        normalise(xall, rows)
        gate = jnp.dot(xn[...], wsin[0], preferred_element_type=F32)
        up = jnp.dot(xn[...], wsin[1], preferred_element_type=F32)
        hidden = (jax.nn.silu(gate) * up).astype(BF16)
        ssa[0, rows, :] = jnp.dot(hidden, wsout[qs], preferred_element_type=F32).astype(BF16)
        ssa[1, rows, :] = jnp.dot(hidden, wsout[qsn], preferred_element_type=F32).astype(BF16)
        spo[rows, :] = jnp.dot(hidden, wsout[q], preferred_element_type=F32)
        spn[rows, :] = jnp.dot(hidden, wsout[qn], preferred_element_type=F32)
        return carry

    lax.fori_loop(0, 2, shared, 0)
    xs = remote(ssa, ssin, xs_s.at[0], xs_r.at[0], gx, sib)
    xs.start()
    xs.wait_recv()

    def fold(c, carry):
        rows = chunk_of(c)
        own = spo[rows, :] + ssin[0, rows, :].astype(F32)
        spo[rows, :] = own
        sb[0, rows, :] = own.astype(BF16)
        sb[1, rows, :] = (spn[rows, :] + ssin[1, rows, :].astype(F32)).astype(BF16)
        return carry

    lax.fori_loop(0, 2, fold, 0)

    def sr(r):
        target = peer(2 * r)
        return remote(
            sb.at[r % 2, :, pl.ds(pl.multiple_of((target // 4) * B, B), B)], shr.at[r],
            sr_s.at[r], sr_r.at[r], gx, target,
        )

    for r in range(1, 8):
        sr(r).start()

    acc[...] = jnp.zeros((TOK, Q), F32)

    def combine(k, carry):
        for u in range(4):
            bk(k, u).wait_recv()
        acc[...] += lax.dot_general(
            og[chunk_of(k), :], back[chunk_of(k), :], (((0,), (0,)), ((), ())), preferred_element_type=F32
        )
        return carry

    lax.fori_loop(0, 4, combine, 0)

    def fn(t):
        return remote(fs.at[t], fin.at[t], fn_s.at[t], fn_r.at[t], gx, peer(4 * t))

    for t in range(1, 4):
        at = pl.multiple_of(((j + t) % 4) * B, B)
        fs[t] = acc[:, pl.ds(at, B)].astype(BF16)
        fn(t).start()
    mine = pl.ds(pl.multiple_of(j * B, B), B)
    total = acc[:, mine] + spo[:, mine]
    for r in range(1, 8):
        sr(r).wait_recv()
        total = total + shr[r].astype(F32)
    for t in range(1, 4):
        fn(t).wait_recv()
        total = total + fin[t].astype(F32)
    out[...] = total.astype(BF16)

    tok_own.wait_send()
    for r in range(1, 8):
        tok_send(r).wait_send()
        tok_forward(r).wait_send()
        sr(r).wait_send()
        for copy in w_ring(r):
            copy.wait_send()
    for e in range(8):
        for copy in w_cross(e):
            copy.wait_send()
    xs.wait_send()
    for t in range(1, 4):
        fn(t).wait_send()

    def drain(k, carry):
        to_nbr(k).wait_send()
        to_sib(0, k).wait_send()
        to_sib(1, k).wait_send()
        ra(k).wait_send()
        rb(k).wait_send()
        for u in range(4):
            def both(u=u):
                dp(k, u).wait_send()
                bk(k, u).wait_send()

            when_self(k, u, lambda: None, both)
        return carry

    lax.fori_loop(0, 4, drain, 0)


def on_device(tokens, norm_gain, expert_ids, gate_weights, shared_in, shared_out, expert_in, expert_out):
    gain = norm_gain.reshape(4, 4, B).transpose(1, 0, 2).reshape(4, 1, Q)
    dma = pltpu.SemaphoreType.DMA
    vmem = pl.BlockSpec(memory_space=pltpu.VMEM)
    anywhere = pl.BlockSpec(memory_space=pl.ANY)
    return pl.pallas_call(
        kernel,
        out_shape=jax.ShapeDtypeStruct((TOK, B), BF16),
        in_specs=[vmem] * 6 + [anywhere] * 2,
        out_specs=vmem,
        scratch_shapes=[
            pltpu.VMEM((4, TOK, Q), BF16),
            pltpu.VMEM((D, 2 * PART), BF16),
            pltpu.VMEM((4, PART, Q), BF16),
            pltpu.VMEM((2, D, SPART), BF16),
            pltpu.VMEM((4, SPART, Q), BF16),
            pltpu.VMEM((NX, TOK), F32),
            pltpu.VMEM((NX, TOK), F32),
            pltpu.VMEM((NX * CAP, TOK), BF16),
            pltpu.VMEM((NX * CAP, TOK), BF16),
            pltpu.VMEM((NX * CAP, Q), BF16),
            pltpu.VMEM((4, NX * CAP, Q), BF16),
            pltpu.VMEM((CH, D), BF16),
            pltpu.VMEM((4, 2, CH, Q), BF16),
            pltpu.VMEM((4, 2, CH, Q), BF16),
            pltpu.VMEM((2, CH, Q), F32),
            pltpu.VMEM((2, CH, Q), F32),
            pltpu.VMEM((4, CH, Q), BF16),
            pltpu.VMEM((4, CH, Q), BF16),
            pltpu.VMEM((NX * CAP, Q), BF16),
            pltpu.VMEM((NX * CAP, Q), BF16),
            pltpu.VMEM((TOK, Q), F32),
            pltpu.VMEM((4, TOK, B), BF16),
            pltpu.VMEM((4, TOK, B), BF16),
            pltpu.VMEM((2, TOK, Q), BF16),
            pltpu.VMEM((2, TOK, Q), BF16),
            pltpu.VMEM((TOK, Q), F32),
            pltpu.VMEM((TOK, Q), F32),
            pltpu.VMEM((2, TOK, Q), BF16),
            pltpu.VMEM((8, TOK, B), BF16),
            dma((2, 16)),
            dma((8,)), dma((8,)),
            dma((8,)), dma((8,)),
            dma((2, 8)), dma((2, 8)),
            dma((2, 8)), dma((2, 8)),
            dma((16,)), dma((16,)),
            dma((4,)), dma((4,)),
            dma((2, 4)), dma((2, 4)),
            dma((4,)), dma((4,)),
            dma((4,)), dma((4,)),
            dma((16,)), dma((16,)),
            dma((1,)), dma((1,)),
            dma((8,)), dma((8,)),
            dma((4,)), dma((4,)),
        ],
        compiler_params=pltpu.CompilerParams(
            collective_id=0, has_side_effects=True, vmem_limit_bytes=VMEM_LIMIT
        ),
    )(
        tokens, gain, expert_ids.T, gate_weights.T, shared_in, shared_out,
        expert_in.reshape(D, 2 * PART), expert_out.reshape(PART, D),
    )


def solution(mesh):
    in_specs = (
        P("gx", "gy"),
        P(),
        P("gx", None),
        P("gx", None),
        P(None, "gx", "gy"),
        P("gy", "gx"),
        P(("gx", "gy"), None, None),
        P(("gx", "gy"), None, None),
    )
    return jax.shard_map(
        on_device, mesh=mesh, in_specs=in_specs, out_specs=P("gx", "gy"), check_vma=False
    )
```

```python
import jax
import jax.numpy as jnp
from jax import lax
from jax.experimental import pallas as pl
from jax.experimental.pallas import tpu as pltpu
from jax.sharding import PartitionSpec as P

MESH = pl.DeviceIdType.MESH
F32 = jnp.float32
BF16 = jnp.bfloat16
EPSILON = 1e-06

NX = 16
NY = 16
CAP = 64
TOK = 512
D = 2048
B = 128
Q = 512
TOPK = 6
PART = 352
SPART = 176
CH = 256
VMEM_LIMIT = 60 * 1024 * 1024


def kernel(
    tok, gain, idst, gatet, shin, shout, win_hbm, wout_hbm, out,
    xall, win, wout, wsin, wsout, code, gm, oh, og, snd, rx, xn, sa, sibin, po, pn, sn, nbrin, ret, back,
    acc, fs, fin, ssa, ssin, spo, spn, sb, shr,
    ld_sem, tok_s, tok_r, tf_s, tf_r, wz_s, wz_r, wy_s, wy_r, dp_s, dp_r, nb_s, nb_r, sq_s, sq_r,
    ra_s, ra_r, rb_s, rb_r, bk_s, bk_r, xs_s, xs_r, sr_s, sr_r, fn_s, fn_r,
):
    gx = lax.axis_index("gx")
    gy = lax.axis_index("gy")
    j, q = gy // 4, gy % 4
    ylo, z = gx // 8, gx % 8
    sib = gy + 1 - 2 * (gy % 2)
    nbr = gy + 2 - 4 * ((gy // 2) % 2)
    qs, qn = sib % 4, nbr % 4
    qsn = (qs + 2) % 4
    ypart = (gx + 8) % NX

    def peer(r):
        return (gy + r) % NY

    def remote(src, dst, send, recv, tx, ty):
        return pltpu.make_async_remote_copy(
            src_ref=src, dst_ref=dst, send_sem=send, recv_sem=recv,
            device_id=(tx, ty), device_id_type=MESH,
        )

    def shift(k, u):
        return 4 * u + (k + 3) % 4

    def loads():
        for i in range(16):
            p = (i % 4) * 4 + i // 4
            yield pltpu.make_async_copy(
                win_hbm.at[:, pl.ds(i * B, B)], win.at[:, pl.ds(p * B, B)], ld_sem.at[0, i]
            )
            yield pltpu.make_async_copy(
                wout_hbm.at[:, pl.ds(i * B, B)], wout.at[i % 4, :, pl.ds((i // 4) * B, B)], ld_sem.at[1, i]
            )

    for copy in loads():
        copy.start()

    barrier = pltpu.get_barrier_semaphore()
    for r in range(1, NX):
        pl.semaphore_signal(barrier, inc=1, device_id=((gx + r) % NX, gy), device_id_type=MESH)
    for r in range(1, 8):
        pl.semaphore_signal(barrier, inc=1, device_id=(gx, peer(2 * r)), device_id_type=MESH)
    pl.semaphore_signal(barrier, inc=1, device_id=(gx, sib), device_id_type=MESH)
    pl.semaphore_wait(barrier, NX - 1 + 8)

    def tok_at(owner):
        return xall.at[owner % 4, :, pl.ds(pl.multiple_of((owner // 4) * B, B), B)]

    def tok_send(r):
        return remote(tok, tok_at(gy), tok_s.at[r], tok_r.at[r], gx, peer(2 * r))

    def tok_recv(r):
        place = tok_at(peer(16 - 2 * r))
        return remote(place, place, tok_s.at[r], tok_r.at[r], gx, sib)

    def tok_forward(r):
        place = tok_at(peer(16 - 2 * r))
        return remote(place, place, tf_s.at[r], tf_r.at[r], gx, sib)

    def tok_forwarded(r):
        place = tok_at((sib + 16 - 2 * r) % NY)
        return remote(place, place, tf_s.at[r], tf_r.at[r], gx, sib)

    tok_own = remote(tok, tok_at(gy), tf_s.at[0], tf_r.at[0], gx, sib)
    for r in (2, 4, 6):
        tok_send(r).start()

    def block_z(e):
        if e == 0:
            return z
        step = (e + 1) // 2
        return (z + 8 - step) % 8 if e % 2 else (z + step) % 8

    def w_at(owner):
        place = (owner % 4) * 4 + owner // 4
        return (
            wsin.at[:, :, pl.ds(pl.multiple_of(place * B, B), B)],
            wsout.at[owner % 4, :, pl.ds(pl.multiple_of((owner // 4) * B, B), B)],
        )

    def w_source(e):
        return (shin, shout) if e == 0 else w_at(ylo * 8 + block_z(e))

    def w_ring(e):
        origin = 0 if e <= 2 else e - 2
        target = ylo * 8 + ((z + 1) % 8 if e % 2 else (z + 7) % 8)
        to = w_at(ylo * 8 + block_z(origin))
        return [
            remote(w_source(origin)[t], to[t], wz_s.at[t, e], wz_r.at[t, e], target, gy) for t in range(2)
        ]

    def w_ring_recv(e):
        place = w_at(ylo * 8 + block_z(e))
        return [remote(place[t], place[t], wz_s.at[t, e], wz_r.at[t, e], ypart, gy) for t in range(2)]

    def w_cross(e):
        to = w_at(ylo * 8 + block_z(e))
        return [remote(w_source(e)[t], to[t], wy_s.at[t, e], wy_r.at[t, e], ypart, gy) for t in range(2)]

    def w_cross_recv(e):
        place = w_at((1 - ylo) * 8 + block_z(e))
        return [remote(place[t], place[t], wy_s.at[t, e], wy_r.at[t, e], ypart, gy) for t in range(2)]

    def start(copies):
        for copy in copies:
            copy.start()

    def arrived(copies):
        for copy in copies:
            copy.wait_recv()

    start(w_ring(1))
    start(w_ring(2))
    tok_own.start()
    for r in (1, 3, 5, 7):
        tok_send(r).start()
    start(w_cross(0))

    xall[q, :, pl.ds(pl.multiple_of(j * B, B), B)] = tok[...]
    wsin[:, :, pl.ds(pl.multiple_of(((gx % 4) * 4 + gx // 4) * B, B), B)] = shin[...]
    wsout[gx % 4, :, pl.ds(pl.multiple_of((gx // 4) * B, B), B)] = shout[...]

    expert = 4 * lax.broadcasted_iota(jnp.int32, (NX, TOK), 0) + j
    named = jnp.zeros((NX, TOK), F32)
    weight = jnp.zeros((NX, TOK), F32)
    for k in range(TOPK):
        hit = idst[k : k + 1, :] == expert
        named = jnp.where(hit, 1.0, named)
        weight = jnp.where(hit, gatet[k : k + 1, :], weight)
    before = (
        lax.broadcasted_iota(jnp.int32, (TOK, TOK), 0) < lax.broadcasted_iota(jnp.int32, (TOK, TOK), 1)
    )
    count = jnp.dot(
        named.astype(BF16), jnp.where(before, 1.0, 0.0).astype(BF16), preferred_element_type=F32
    )
    code[...] = jnp.where(named > 0.0, count, -1.0)
    gm[...] = weight
    slot = lax.broadcasted_iota(jnp.int32, (CAP, TOK), 0).astype(F32)

    def build(k, carry):
        for u in range(4):
            m = (gx + shift(k, u)) % NX
            hit = slot == code[pl.ds(m, 1), :]
            at = pl.multiple_of((4 * k + u) * CAP, CAP)
            oh[pl.ds(at, CAP), :] = jnp.where(hit, 1.0, 0.0).astype(BF16)
            og[pl.ds(at, CAP), :] = jnp.where(hit, gm[pl.ds(m, 1), :], 0.0).astype(BF16)
        return carry

    lax.fori_loop(0, 4, build, 0)

    def slots_of(k, u):
        return pl.ds(pl.multiple_of((4 * k + u) * CAP, CAP), CAP)

    def chunk_of(k):
        return pl.ds(pl.multiple_of(k * CH, CH), CH)

    def dp(k, u):
        return remote(
            snd.at[slots_of(k, u), :], rx.at[q, slots_of(k, u), :],
            dp_s.at[4 * k + u], dp_r.at[4 * k + u], (gx + shift(k, u)) % NX, gy,
        )

    def when_self(k, u, own, other):
        if u == 0:
            pl.when(k == 1)(own)
            pl.when(k != 1)(other)
        else:
            other()

    for r in (2, 4, 6):
        tok_recv(r).wait_recv()

    def dispatch(k, carry):
        picked = jnp.dot(oh[chunk_of(k), :], xall[q], preferred_element_type=F32)
        snd[chunk_of(k), :] = picked.astype(BF16)
        for u in range(4):
            def own(u=u):
                pltpu.make_async_copy(
                    snd.at[slots_of(k, u), :], rx.at[q, slots_of(k, u), :], dp_r.at[4 * k + u]
                ).start()

            when_self(k, u, own, lambda u=u: dp(k, u).start())
        return carry

    lax.fori_loop(0, 4, dispatch, 0)

    for e in (1, 2):
        arrived(w_ring_recv(e))
        start(w_ring(e + 2))
        start(w_cross(e))
    for r in (2, 4, 6):
        tok_forward(r).start()
    for r in (1, 3, 5, 7):
        tok_recv(r).wait_recv()
        tok_forward(r).start()
    for e in (3, 4):
        arrived(w_ring_recv(e))
        start(w_ring(e + 2))
        start(w_cross(e))

    def to_nbr(k):
        place = rx.at[q, chunk_of(k), :]
        return remote(place, place, nb_s.at[k], nb_r.at[k], gx, nbr)

    def from_nbr(k):
        place = rx.at[qn, chunk_of(k), :]
        return remote(place, place, nb_s.at[k], nb_r.at[k], gx, nbr)

    def to_sib(t, k):
        place = rx.at[q if t == 0 else qn, chunk_of(k), :]
        return remote(place, place, sq_s.at[t, k], sq_r.at[t, k], gx, sib)

    def from_sib(t, k):
        place = rx.at[qs if t == 0 else qsn, chunk_of(k), :]
        return remote(place, place, sq_s.at[t, k], sq_r.at[t, k], gx, sib)

    def stage_a(k):
        for u in range(4):
            place = rx.at[q, slots_of(k, u), :]
            remote(place, place, dp_s.at[4 * k + u], dp_r.at[4 * k + u], gx, sib).wait_recv()
        to_nbr(k).start()
        to_sib(0, k).start()

    def stage_a2(k):
        from_nbr(k).wait_recv()
        to_sib(1, k).start()

    def ra(k):
        return remote(sa.at[k], sibin.at[k], ra_s.at[k], ra_r.at[k], gx, sib)

    def rb(k):
        return remote(sn.at[k], nbrin.at[k], rb_s.at[k], rb_r.at[k], gx, nbr)

    def bk(k, u):
        return remote(
            ret.at[slots_of(k, u), :], back.at[slots_of(k, u), :],
            bk_s.at[4 * k + u], bk_r.at[4 * k + u], (gx + NX - shift(k, u)) % NX, gy,
        )

    def dot_nt(a, b):
        return lax.dot_general(a, b, (((1,), (1,)), ((), ())), preferred_element_type=F32)

    def normalise(source, rows):
        total = jnp.zeros((CH, B), F32)
        for c in range(4):
            for b in range(4):
                value = source[c, rows, b * B : (b + 1) * B].astype(F32)
                total = total + value * value
        inverse = lax.rsqrt(jnp.sum(total, axis=1, keepdims=True) * (1.0 / D) + EPSILON)
        for c in range(4):
            for b in range(4):
                value = source[c, rows, b * B : (b + 1) * B].astype(F32)
                scaled = value * inverse * gain[4 * b + c : 4 * b + c + 1, :]
                xn[:, c * Q + b * B : c * Q + (b + 1) * B] = scaled.astype(BF16)

    def stage_b(k):
        from_sib(0, k).wait_recv()
        from_sib(1, k).wait_recv()
        normalise(rx, chunk_of(k))
        gate, up = dot_nt(xn[...], win[:PART, :]), dot_nt(xn[...], win[PART:, :])
        hidden = (jax.nn.silu(gate) * up).astype(BF16)
        sa[k, 0] = jnp.dot(hidden, wout[qs], preferred_element_type=F32).astype(BF16)
        sa[k, 1] = jnp.dot(hidden, wout[qsn], preferred_element_type=F32).astype(BF16)
        ra(k).start()
        pn[k % 2] = jnp.dot(hidden, wout[qn], preferred_element_type=F32)
        po[k % 2] = jnp.dot(hidden, wout[q], preferred_element_type=F32)

    def stage_rb(k):
        remote(sa.at[k], sibin.at[k], ra_s.at[k], ra_r.at[k], gx, sib).wait_recv()
        sn[k] = (pn[k % 2] + sibin[k, 1].astype(F32)).astype(BF16)
        rb(k).start()
        po[k % 2] = po[k % 2] + sibin[k, 0].astype(F32)

    def stage_c(k):
        remote(sn.at[k], nbrin.at[k], rb_s.at[k], rb_r.at[k], gx, nbr).wait_recv()
        ret[chunk_of(k), :] = (po[k % 2] + nbrin[k].astype(F32)).astype(BF16)
        for u in range(4):
            def own(u=u):
                pltpu.make_async_copy(
                    ret.at[slots_of(k, u), :], back.at[slots_of(k, u), :], bk_r.at[4 * k + u]
                ).start()

            when_self(k, u, own, lambda u=u: bk(k, u).start())

    stage_a(0)
    for e in (5, 6):
        arrived(w_ring_recv(e))
        if e == 5:
            start(w_ring(7))
        start(w_cross(e))
    for copy in loads():
        copy.wait()

    def routed(it, carry):
        @pl.when(it < 3)
        def _():
            stage_a(it + 1)

        @pl.when(it < 4)
        def _():
            stage_a2(it)

        @pl.when(it > 0)
        def _():
            stage_rb(it - 1)

        @pl.when(it < 4)
        def _():
            stage_b(it)

        @pl.when(it > 0)
        def _():
            stage_c(it - 1)

        return carry

    lax.fori_loop(0, 5, routed, 0)

    arrived(w_ring_recv(7))
    start(w_cross(7))
    tok_forwarded(0).wait_recv()
    for r in range(1, 8):
        tok_forwarded(r).wait_recv()
    for e in range(8):
        arrived(w_cross_recv(e))

    def shared(c, carry):
        rows = chunk_of(c)
        normalise(xall, rows)
        gate, up = dot_nt(xn[...], wsin[0]), dot_nt(xn[...], wsin[1])
        hidden = (jax.nn.silu(gate) * up).astype(BF16)
        ssa[0, rows, :] = jnp.dot(hidden, wsout[qs], preferred_element_type=F32).astype(BF16)
        ssa[1, rows, :] = jnp.dot(hidden, wsout[qsn], preferred_element_type=F32).astype(BF16)
        spo[rows, :] = jnp.dot(hidden, wsout[q], preferred_element_type=F32)
        spn[rows, :] = jnp.dot(hidden, wsout[qn], preferred_element_type=F32)
        return carry

    lax.fori_loop(0, 2, shared, 0)
    xs = remote(ssa, ssin, xs_s.at[0], xs_r.at[0], gx, sib)
    xs.start()
    xs.wait_recv()

    def fold(c, carry):
        rows = chunk_of(c)
        own = spo[rows, :] + ssin[0, rows, :].astype(F32)
        spo[rows, :] = own
        sb[0, rows, :] = own.astype(BF16)
        sb[1, rows, :] = (spn[rows, :] + ssin[1, rows, :].astype(F32)).astype(BF16)
        return carry

    lax.fori_loop(0, 2, fold, 0)

    def sr(r):
        target = peer(2 * r)
        return remote(
            sb.at[r % 2, :, pl.ds(pl.multiple_of((target // 4) * B, B), B)], shr.at[r],
            sr_s.at[r], sr_r.at[r], gx, target,
        )

    for r in range(1, 8):
        sr(r).start()

    acc[...] = jnp.zeros((TOK, Q), F32)

    def combine(k, carry):
        for u in range(4):
            bk(k, u).wait_recv()
        acc[...] += lax.dot_general(
            og[chunk_of(k), :], back[chunk_of(k), :], (((0,), (0,)), ((), ())), preferred_element_type=F32
        )
        return carry

    lax.fori_loop(0, 4, combine, 0)

    def fn(t):
        return remote(fs.at[t], fin.at[t], fn_s.at[t], fn_r.at[t], gx, peer(4 * t))

    for t in range(1, 4):
        at = pl.multiple_of(((j + t) % 4) * B, B)
        fs[t] = acc[:, pl.ds(at, B)].astype(BF16)
        fn(t).start()
    mine = pl.ds(pl.multiple_of(j * B, B), B)
    total = acc[:, mine] + spo[:, mine]
    for r in range(1, 8):
        sr(r).wait_recv()
        total = total + shr[r].astype(F32)
    for t in range(1, 4):
        fn(t).wait_recv()
        total = total + fin[t].astype(F32)
    out[...] = total.astype(BF16)

    tok_own.wait_send()
    for r in range(1, 8):
        tok_send(r).wait_send()
        tok_forward(r).wait_send()
        sr(r).wait_send()
        for copy in w_ring(r):
            copy.wait_send()
    for e in range(8):
        for copy in w_cross(e):
            copy.wait_send()
    xs.wait_send()
    for t in range(1, 4):
        fn(t).wait_send()

    def drain(k, carry):
        to_nbr(k).wait_send()
        to_sib(0, k).wait_send()
        to_sib(1, k).wait_send()
        ra(k).wait_send()
        rb(k).wait_send()
        for u in range(4):
            def both(u=u):
                dp(k, u).wait_send()
                bk(k, u).wait_send()

            when_self(k, u, lambda: None, both)
        return carry

    lax.fori_loop(0, 4, drain, 0)


def on_device(tokens, norm_gain, expert_ids, gate_weights, shared_in, shared_out, expert_in, expert_out):
    dma = pltpu.SemaphoreType.DMA
    vmem = pl.BlockSpec(memory_space=pltpu.VMEM)
    anywhere = pl.BlockSpec(memory_space=pl.ANY)
    return pl.pallas_call(
        kernel,
        out_shape=jax.ShapeDtypeStruct((TOK, B), BF16),
        in_specs=[vmem] * 6 + [anywhere] * 2,
        out_specs=vmem,
        scratch_shapes=[
            pltpu.VMEM((4, TOK, Q), BF16),
            pltpu.VMEM((2 * PART, D), BF16),
            pltpu.VMEM((4, PART, Q), BF16),
            pltpu.VMEM((2, SPART, D), BF16),
            pltpu.VMEM((4, SPART, Q), BF16),
            pltpu.VMEM((NX, TOK), F32),
            pltpu.VMEM((NX, TOK), F32),
            pltpu.VMEM((NX * CAP, TOK), BF16),
            pltpu.VMEM((NX * CAP, TOK), BF16),
            pltpu.VMEM((NX * CAP, Q), BF16),
            pltpu.VMEM((4, NX * CAP, Q), BF16),
            pltpu.VMEM((CH, D), BF16),
            pltpu.VMEM((4, 2, CH, Q), BF16),
            pltpu.VMEM((4, 2, CH, Q), BF16),
            pltpu.VMEM((2, CH, Q), F32),
            pltpu.VMEM((2, CH, Q), F32),
            pltpu.VMEM((4, CH, Q), BF16),
            pltpu.VMEM((4, CH, Q), BF16),
            pltpu.VMEM((NX * CAP, Q), BF16),
            pltpu.VMEM((NX * CAP, Q), BF16),
            pltpu.VMEM((TOK, Q), F32),
            pltpu.VMEM((4, TOK, B), BF16),
            pltpu.VMEM((4, TOK, B), BF16),
            pltpu.VMEM((2, TOK, Q), BF16),
            pltpu.VMEM((2, TOK, Q), BF16),
            pltpu.VMEM((TOK, Q), F32),
            pltpu.VMEM((TOK, Q), F32),
            pltpu.VMEM((2, TOK, Q), BF16),
            pltpu.VMEM((8, TOK, B), BF16),
            dma((2, 16)),
            dma((8,)), dma((8,)),
            dma((8,)), dma((8,)),
            dma((2, 8)), dma((2, 8)),
            dma((2, 8)), dma((2, 8)),
            dma((16,)), dma((16,)),
            dma((4,)), dma((4,)),
            dma((2, 4)), dma((2, 4)),
            dma((4,)), dma((4,)),
            dma((4,)), dma((4,)),
            dma((16,)), dma((16,)),
            dma((1,)), dma((1,)),
            dma((8,)), dma((8,)),
            dma((4,)), dma((4,)),
        ],
        compiler_params=pltpu.CompilerParams(
            collective_id=0, has_side_effects=True, vmem_limit_bytes=VMEM_LIMIT
        ),
    )(
        tokens, norm_gain.reshape(D // B, B), expert_ids.T, gate_weights.T,
        jnp.swapaxes(shared_in, 1, 2), shared_out,
        expert_in.reshape(D, 2 * PART).T, expert_out.reshape(PART, D),
    )


def solution(mesh):
    in_specs = (
        P("gx", "gy"),
        P(),
        P("gx", None),
        P("gx", None),
        P(None, "gx", "gy"),
        P("gy", "gx"),
        P(("gx", "gy"), None, None),
        P(("gx", "gy"), None, None),
    )
    return jax.shard_map(
        on_device, mesh=mesh, in_specs=in_specs, out_specs=P("gx", "gy"), check_vma=False
    )
```

```python
import jax
import jax.numpy as jnp
from jax import lax
from jax.experimental import pallas as pl
from jax.experimental.pallas import tpu as pltpu
from jax.sharding import PartitionSpec as P

MESH = pl.DeviceIdType.MESH
F32 = jnp.float32
BF16 = jnp.bfloat16
EPSILON = 1e-06

NX = 16
NY = 16
CAP = 64
TOK = 512
D = 2048
B = 128
Q = 512
TOPK = 6
PART = 352
SPART = 176
NS = 2
NC = NX // NS
CH = NS * CAP
SELF = 4 if NS == 2 else 1
SH = 256
VMEM_LIMIT = 60 * 1024 * 1024


def kernel(
    tok, gain, idst, gatet, shin, shout, win_hbm, wout_hbm, out,
    xall, win, wout, wsin, wsout, code, gm, oh, og, snd, rx, xn, sa, sibin, po, pn, sn, nbrin, ret, back,
    acc, fs, fin, ssa, ssin, spo, spn, sb, shr,
    ld_sem, tok_s, tok_r, tf_s, tf_r, wz_s, wz_r, wy_s, wy_r, dp_s, dp_r, nb_s, nb_r, sq_s, sq_r,
    ra_s, ra_r, rb_s, rb_r, bk_s, bk_r, xs_s, xs_r, sr_s, sr_r, fn_s, fn_r,
):
    gx = lax.axis_index("gx")
    gy = lax.axis_index("gy")
    j, q = gy // 4, gy % 4
    ylo, z = gx // 8, gx % 8
    sib = gy + 1 - 2 * (gy % 2)
    nbr = gy + 2 - 4 * ((gy // 2) % 2)
    qs, qn = sib % 4, nbr % 4
    qsn = (qs + 2) % 4
    ypart = (gx + 8) % NX

    def peer(r):
        return (gy + r) % NY

    def remote(src, dst, send, recv, tx, ty):
        return pltpu.make_async_remote_copy(
            src_ref=src, dst_ref=dst, send_sem=send, recv_sem=recv,
            device_id=(tx, ty), device_id_type=MESH,
        )

    def shift(k, u):
        return 8 * u + (3 * k + 4) % 8 if NS == 2 else 4 * u + (k + 3) % 4

    def loads():
        for i in range(16):
            p = (i % 4) * 4 + i // 4
            yield pltpu.make_async_copy(
                win_hbm.at[:, pl.ds(i * B, B)], win.at[:, pl.ds(p * B, B)], ld_sem.at[0, i]
            )
            yield pltpu.make_async_copy(
                wout_hbm.at[:, pl.ds(i * B, B)], wout.at[i % 4, :, pl.ds((i // 4) * B, B)], ld_sem.at[1, i]
            )

    for copy in loads():
        copy.start()

    barrier = pltpu.get_barrier_semaphore()
    for r in range(1, NX):
        pl.semaphore_signal(barrier, inc=1, device_id=((gx + r) % NX, gy), device_id_type=MESH)
    for r in range(1, 8):
        pl.semaphore_signal(barrier, inc=1, device_id=(gx, peer(2 * r)), device_id_type=MESH)
    pl.semaphore_signal(barrier, inc=1, device_id=(gx, sib), device_id_type=MESH)

    expert = 4 * lax.broadcasted_iota(jnp.int32, (NX, TOK), 0) + j
    named = jnp.zeros((NX, TOK), F32)
    weight = jnp.zeros((NX, TOK), F32)
    for k in range(TOPK):
        hit = idst[k : k + 1, :] == expert
        named = jnp.where(hit, 1.0, named)
        weight = jnp.where(hit, gatet[k : k + 1, :], weight)
    before = (
        lax.broadcasted_iota(jnp.int32, (TOK, TOK), 0) < lax.broadcasted_iota(jnp.int32, (TOK, TOK), 1)
    )
    count = jnp.dot(
        named.astype(BF16), jnp.where(before, 1.0, 0.0).astype(BF16), preferred_element_type=F32
    )
    code[...] = jnp.where(named > 0.0, count, -1.0)
    gm[...] = weight
    slot = lax.broadcasted_iota(jnp.int32, (CAP, TOK), 0).astype(F32)

    def build(k, carry):
        for u in range(NS):
            m = (gx + shift(k, u)) % NX
            hit = slot == code[pl.ds(m, 1), :]
            at = pl.multiple_of((NS * k + u) * CAP, CAP)
            oh[pl.ds(at, CAP), :] = jnp.where(hit, 1.0, 0.0).astype(BF16)
            og[pl.ds(at, CAP), :] = jnp.where(hit, gm[pl.ds(m, 1), :], 0.0).astype(BF16)
        return carry

    lax.fori_loop(0, NC, build, 0)

    pl.semaphore_wait(barrier, NX - 1 + 8)

    def tok_at(owner):
        return xall.at[owner % 4, :, pl.ds(pl.multiple_of((owner // 4) * B, B), B)]

    def tok_send(r):
        return remote(tok, tok_at(gy), tok_s.at[r], tok_r.at[r], gx, peer(2 * r))

    def tok_recv(r):
        place = tok_at(peer(16 - 2 * r))
        return remote(place, place, tok_s.at[r], tok_r.at[r], gx, sib)

    def tok_forward(r):
        place = tok_at(peer(16 - 2 * r))
        return remote(place, place, tf_s.at[r], tf_r.at[r], gx, sib)

    def tok_forwarded(r):
        place = tok_at((sib + 16 - 2 * r) % NY)
        return remote(place, place, tf_s.at[r], tf_r.at[r], gx, sib)

    tok_own = remote(tok, tok_at(gy), tf_s.at[0], tf_r.at[0], gx, sib)
    for r in (2, 4, 6):
        tok_send(r).start()

    def block_z(e):
        if e == 0:
            return z
        step = (e + 1) // 2
        return (z + 8 - step) % 8 if e % 2 else (z + step) % 8

    def w_at(owner):
        place = (owner % 4) * 4 + owner // 4
        return (
            wsin.at[:, :, pl.ds(pl.multiple_of(place * B, B), B)],
            wsout.at[owner % 4, :, pl.ds(pl.multiple_of((owner // 4) * B, B), B)],
        )

    def w_source(e):
        return (shin, shout) if e == 0 else w_at(ylo * 8 + block_z(e))

    def w_ring(e):
        origin = 0 if e <= 2 else e - 2
        target = ylo * 8 + ((z + 1) % 8 if e % 2 else (z + 7) % 8)
        to = w_at(ylo * 8 + block_z(origin))
        return [
            remote(w_source(origin)[t], to[t], wz_s.at[t, e], wz_r.at[t, e], target, gy) for t in range(2)
        ]

    def w_ring_recv(e):
        place = w_at(ylo * 8 + block_z(e))
        return [remote(place[t], place[t], wz_s.at[t, e], wz_r.at[t, e], ypart, gy) for t in range(2)]

    def w_cross(e):
        to = w_at(ylo * 8 + block_z(e))
        return [remote(w_source(e)[t], to[t], wy_s.at[t, e], wy_r.at[t, e], ypart, gy) for t in range(2)]

    def w_cross_recv(e):
        place = w_at((1 - ylo) * 8 + block_z(e))
        return [remote(place[t], place[t], wy_s.at[t, e], wy_r.at[t, e], ypart, gy) for t in range(2)]

    def start(copies):
        for copy in copies:
            copy.start()

    def arrived(copies):
        for copy in copies:
            copy.wait_recv()

    start(w_ring(1))
    start(w_ring(2))
    tok_own.start()
    for r in (1, 3, 5, 7):
        tok_send(r).start()
    start(w_cross(0))

    xall[q, :, pl.ds(pl.multiple_of(j * B, B), B)] = tok[...]
    wsin[:, :, pl.ds(pl.multiple_of(((gx % 4) * 4 + gx // 4) * B, B), B)] = shin[...]
    wsout[gx % 4, :, pl.ds(pl.multiple_of((gx // 4) * B, B), B)] = shout[...]

    def slots_of(k, u):
        return pl.ds(pl.multiple_of((NS * k + u) * CAP, CAP), CAP)

    def chunk_of(k):
        return pl.ds(pl.multiple_of(k * CH, CH), CH)

    def dp(k, u):
        return remote(
            snd.at[slots_of(k, u), :], rx.at[q, slots_of(k, u), :],
            dp_s.at[NS * k + u], dp_r.at[NS * k + u], (gx + shift(k, u)) % NX, gy,
        )

    def when_self(k, u, own, other):
        if u == 0:
            pl.when(k == SELF)(own)
            pl.when(k != SELF)(other)
        else:
            other()

    for e in (1, 2):
        arrived(w_ring_recv(e))
        start(w_ring(e + 2))
    for r in (2, 4, 6):
        tok_recv(r).wait_recv()

    def dispatch(k, carry):
        picked = jnp.dot(oh[chunk_of(k), :], xall[q], preferred_element_type=F32)
        snd[chunk_of(k), :] = picked.astype(BF16)
        for u in range(NS):
            def own(u=u):
                pltpu.make_async_copy(
                    snd.at[slots_of(k, u), :], rx.at[q, slots_of(k, u), :], dp_r.at[NS * k + u]
                ).start()

            when_self(k, u, own, lambda u=u: dp(k, u).start())
        return carry

    lax.fori_loop(0, NC, dispatch, 0)

    def to_nbr(k):
        place = rx.at[q, chunk_of(k), :]
        return remote(place, place, nb_s.at[k], nb_r.at[k], gx, nbr)

    def from_nbr(k):
        place = rx.at[qn, chunk_of(k), :]
        return remote(place, place, nb_s.at[k], nb_r.at[k], gx, nbr)

    def to_sib(t, k):
        place = rx.at[q if t == 0 else qn, chunk_of(k), :]
        return remote(place, place, sq_s.at[t, k], sq_r.at[t, k], gx, sib)

    def from_sib(t, k):
        place = rx.at[qs if t == 0 else qsn, chunk_of(k), :]
        return remote(place, place, sq_s.at[t, k], sq_r.at[t, k], gx, sib)

    def stage_a(k):
        for u in range(NS):
            place = rx.at[q, slots_of(k, u), :]
            remote(place, place, dp_s.at[NS * k + u], dp_r.at[NS * k + u], gx, sib).wait_recv()
        to_nbr(k).start()
        to_sib(0, k).start()

    def stage_a2(k):
        from_nbr(k).wait_recv()
        to_sib(1, k).start()

    def ra(k):
        return remote(sa.at[k], sibin.at[k], ra_s.at[k], ra_r.at[k], gx, sib)

    def rb(k):
        return remote(sn.at[k], nbrin.at[k], rb_s.at[k], rb_r.at[k], gx, nbr)

    def bk(k, u):
        return remote(
            ret.at[slots_of(k, u), :], back.at[slots_of(k, u), :],
            bk_s.at[NS * k + u], bk_r.at[NS * k + u], (gx + NX - shift(k, u)) % NX, gy,
        )

    def dot_nt(a, b):
        return lax.dot_general(a, b, (((1,), (1,)), ((), ())), preferred_element_type=F32)

    def normalise(source, rows, size):
        total = jnp.zeros((size, B), F32)
        for c in range(4):
            for b in range(4):
                value = source[c, rows, b * B : (b + 1) * B].astype(F32)
                total = total + value * value
        inverse = lax.rsqrt(jnp.sum(total, axis=1, keepdims=True) * (1.0 / D) + EPSILON)
        for c in range(4):
            for b in range(4):
                value = source[c, rows, b * B : (b + 1) * B].astype(F32)
                scaled = value * inverse * gain[4 * b + c : 4 * b + c + 1, :]
                xn[:size, c * Q + b * B : c * Q + (b + 1) * B] = scaled.astype(BF16)

    def stage_b(k):
        from_sib(0, k).wait_recv()
        from_sib(1, k).wait_recv()
        normalise(rx, chunk_of(k), CH)
        gate, up = dot_nt(xn[:CH, :], win[:PART, :]), dot_nt(xn[:CH, :], win[PART:, :])
        hidden = (jax.nn.silu(gate) * up).astype(BF16)
        sa[k, 0] = jnp.dot(hidden, wout[qs], preferred_element_type=F32).astype(BF16)
        sa[k, 1] = jnp.dot(hidden, wout[qsn], preferred_element_type=F32).astype(BF16)
        ra(k).start()
        pn[k] = jnp.dot(hidden, wout[qn], preferred_element_type=F32)
        po[k] = jnp.dot(hidden, wout[q], preferred_element_type=F32)

    def stage_rb(k):
        remote(sa.at[k], sibin.at[k], ra_s.at[k], ra_r.at[k], gx, sib).wait_recv()
        sn[k] = (pn[k] + sibin[k, 1].astype(F32)).astype(BF16)
        rb(k).start()
        po[k] = po[k] + sibin[k, 0].astype(F32)

    def stage_c(k):
        remote(sn.at[k], nbrin.at[k], rb_s.at[k], rb_r.at[k], gx, nbr).wait_recv()
        ret[chunk_of(k), :] = (po[k] + nbrin[k].astype(F32)).astype(BF16)
        for u in range(NS):
            def own(u=u):
                pltpu.make_async_copy(
                    ret.at[slots_of(k, u), :], back.at[slots_of(k, u), :], bk_r.at[NS * k + u]
                ).start()

            when_self(k, u, own, lambda u=u: bk(k, u).start())

    def ring_a():
        for e in (3, 4):
            arrived(w_ring_recv(e))
            start(w_ring(e + 2))
        for e in (1, 2):
            start(w_cross(e))

    def ring_b():
        for e in (5, 6):
            arrived(w_ring_recv(e))
        start(w_ring(7))
        for e in (3, 4):
            start(w_cross(e))

    def ring_c():
        arrived(w_ring_recv(7))
        for e in (5, 6, 7):
            start(w_cross(e))

    def others():
        for r in (2, 4, 6):
            tok_forward(r).start()
        for r in (1, 3, 5, 7):
            tok_recv(r).wait_recv()
            tok_forward(r).start()

    AHEAD = 2 if NS == 2 else 1
    for k in range(AHEAD):
        stage_a(k)
    others()
    ring_a()
    stage_a2(0)
    for copy in loads():
        copy.wait()

    def routed(it, carry):
        @pl.when(it < NC - AHEAD)
        def _():
            stage_a(it + AHEAD)

        @pl.when(it < NC - 1)
        def _():
            stage_a2(it + 1)

        stage_b(it)

        @pl.when(it > 0)
        def _():
            stage_rb(it - 1)

        pl.when(it == NC // 4)(ring_b)
        pl.when(it == NC // 2)(ring_c)
        return carry

    lax.fori_loop(0, NC, routed, 0)
    stage_rb(NC - 1)

    def rows_of(c):
        return pl.ds(pl.multiple_of(c * SH, SH), SH)

    tok_forwarded(0).wait_recv()
    for r in range(1, 8):
        tok_forwarded(r).wait_recv()
    for e in range(8):
        arrived(w_cross_recv(e))

    def xs(c):
        return remote(ssa.at[c], ssin.at[c], xs_s.at[c], xs_r.at[c], gx, sib)

    def sr(c, r):
        target = peer(2 * r)
        return remote(
            sb.at[r % 2, rows_of(c), pl.ds(pl.multiple_of((target // 4) * B, B), B)], shr.at[r, rows_of(c), :],
            sr_s.at[c, r], sr_r.at[c, r], gx, target,
        )

    def shared(c):
        rows = rows_of(c)
        normalise(xall, rows, SH)
        gate, up = dot_nt(xn[...], wsin[0]), dot_nt(xn[...], wsin[1])
        hidden = (jax.nn.silu(gate) * up).astype(BF16)
        ssa[c, 0] = jnp.dot(hidden, wsout[qs], preferred_element_type=F32).astype(BF16)
        ssa[c, 1] = jnp.dot(hidden, wsout[qsn], preferred_element_type=F32).astype(BF16)
        xs(c).start()
        spo[rows, :] = jnp.dot(hidden, wsout[q], preferred_element_type=F32)
        spn[rows, :] = jnp.dot(hidden, wsout[qn], preferred_element_type=F32)

    def fold(c):
        rows = rows_of(c)
        xs(c).wait_recv()
        own = spo[rows, :] + ssin[c, 0].astype(F32)
        spo[rows, :] = own
        sb[0, rows, :] = own.astype(BF16)
        sb[1, rows, :] = (spn[rows, :] + ssin[c, 1].astype(F32)).astype(BF16)
        for r in range(1, 8):
            sr(c, r).start()

    STEP = NC // 4

    def finish(k, carry):
        stage_c(k)
        part = k // STEP
        pl.when((k % STEP == STEP - 1) & (part % 2 == 0))(lambda: shared(part // 2))
        pl.when((k % STEP == STEP - 1) & (part % 2 == 1))(lambda: fold(part // 2))
        return carry

    lax.fori_loop(0, NC, finish, 0)

    acc[...] = jnp.zeros((TOK, Q), F32)

    def combine(k, carry):
        for u in range(4):
            i = 4 * k + u
            bk(i // NS, i % NS).wait_recv()
        rows = rows_of(k)
        acc[...] += lax.dot_general(
            og[rows, :], back[rows, :], (((0,), (0,)), ((), ())), preferred_element_type=F32
        )
        return carry

    lax.fori_loop(0, 4, combine, 0)

    def fn(t):
        return remote(fs.at[t], fin.at[t], fn_s.at[t], fn_r.at[t], gx, peer(4 * t))

    for t in range(1, 4):
        at = pl.multiple_of(((j + t) % 4) * B, B)
        fs[t] = acc[:, pl.ds(at, B)].astype(BF16)
        fn(t).start()
    mine = pl.ds(pl.multiple_of(j * B, B), B)
    total = acc[:, mine] + spo[:, mine]
    for r in range(1, 8):
        for c in range(2):
            sr(c, r).wait_recv()
        total = total + shr[r].astype(F32)
    for t in range(1, 4):
        fn(t).wait_recv()
        total = total + fin[t].astype(F32)
    out[...] = total.astype(BF16)

    tok_own.wait_send()
    for r in range(1, 8):
        tok_send(r).wait_send()
        tok_forward(r).wait_send()
        for c in range(2):
            sr(c, r).wait_send()
        for copy in w_ring(r):
            copy.wait_send()
    for e in range(8):
        for copy in w_cross(e):
            copy.wait_send()
    for c in range(2):
        xs(c).wait_send()
    for t in range(1, 4):
        fn(t).wait_send()

    def drain(k, carry):
        to_nbr(k).wait_send()
        to_sib(0, k).wait_send()
        to_sib(1, k).wait_send()
        ra(k).wait_send()
        rb(k).wait_send()
        for u in range(NS):
            def both(u=u):
                dp(k, u).wait_send()
                bk(k, u).wait_send()

            when_self(k, u, lambda: None, both)
        return carry

    lax.fori_loop(0, NC, drain, 0)


def on_device(tokens, norm_gain, expert_ids, gate_weights, shared_in, shared_out, expert_in, expert_out):
    dma = pltpu.SemaphoreType.DMA
    vmem = pl.BlockSpec(memory_space=pltpu.VMEM)
    anywhere = pl.BlockSpec(memory_space=pl.ANY)
    return pl.pallas_call(
        kernel,
        out_shape=jax.ShapeDtypeStruct((TOK, B), BF16),
        in_specs=[vmem] * 6 + [anywhere] * 2,
        out_specs=vmem,
        scratch_shapes=[
            pltpu.VMEM((4, TOK, Q), BF16),
            pltpu.VMEM((2 * PART, D), BF16),
            pltpu.VMEM((4, PART, Q), BF16),
            pltpu.VMEM((2, SPART, D), BF16),
            pltpu.VMEM((4, SPART, Q), BF16),
            pltpu.VMEM((NX, TOK), F32),
            pltpu.VMEM((NX, TOK), F32),
            pltpu.VMEM((NX * CAP, TOK), BF16),
            pltpu.VMEM((NX * CAP, TOK), BF16),
            pltpu.VMEM((NX * CAP, Q), BF16),
            pltpu.VMEM((4, NX * CAP, Q), BF16),
            pltpu.VMEM((SH, D), BF16),
            pltpu.VMEM((NC, 2, CH, Q), BF16),
            pltpu.VMEM((NC, 2, CH, Q), BF16),
            pltpu.VMEM((NC, CH, Q), F32),
            pltpu.VMEM((NC, CH, Q), F32),
            pltpu.VMEM((NC, CH, Q), BF16),
            pltpu.VMEM((NC, CH, Q), BF16),
            pltpu.VMEM((NX * CAP, Q), BF16),
            pltpu.VMEM((NX * CAP, Q), BF16),
            pltpu.VMEM((TOK, Q), F32),
            pltpu.VMEM((4, TOK, B), BF16),
            pltpu.VMEM((4, TOK, B), BF16),
            pltpu.VMEM((2, 2, SH, Q), BF16),
            pltpu.VMEM((2, 2, SH, Q), BF16),
            pltpu.VMEM((TOK, Q), F32),
            pltpu.VMEM((TOK, Q), F32),
            pltpu.VMEM((2, TOK, Q), BF16),
            pltpu.VMEM((8, TOK, B), BF16),
            dma((2, 16)),
            dma((8,)), dma((8,)),
            dma((8,)), dma((8,)),
            dma((2, 8)), dma((2, 8)),
            dma((2, 8)), dma((2, 8)),
            dma((16,)), dma((16,)),
            dma((NC,)), dma((NC,)),
            dma((2, NC)), dma((2, NC)),
            dma((NC,)), dma((NC,)),
            dma((NC,)), dma((NC,)),
            dma((16,)), dma((16,)),
            dma((2,)), dma((2,)),
            dma((2, 8)), dma((2, 8)),
            dma((4,)), dma((4,)),
        ],
        compiler_params=pltpu.CompilerParams(
            collective_id=0, has_side_effects=True, vmem_limit_bytes=VMEM_LIMIT
        ),
    )(
        tokens, norm_gain.reshape(D // B, B), expert_ids.T, gate_weights.T,
        jnp.swapaxes(shared_in, 1, 2), shared_out,
        expert_in.reshape(D, 2 * PART).T, expert_out.reshape(PART, D),
    )


def solution(mesh):
    in_specs = (
        P("gx", "gy"),
        P(),
        P("gx", None),
        P("gx", None),
        P(None, "gx", "gy"),
        P("gy", "gx"),
        P(("gx", "gy"), None, None),
        P(("gx", "gy"), None, None),
    )
    return jax.shard_map(
        on_device, mesh=mesh, in_specs=in_specs, out_specs=P("gx", "gy"), check_vma=False
    )
```

```python
import jax
import jax.numpy as jnp
from jax import lax
from jax.experimental import pallas as pl
from jax.experimental.pallas import tpu as pltpu
from jax.sharding import PartitionSpec as P

MESH = pl.DeviceIdType.MESH
F32 = jnp.float32
BF16 = jnp.bfloat16
EPSILON = 1e-06

NX = 16
NY = 16
CAP = 64
TOK = 512
D = 2048
B = 128
Q = 512
TOPK = 6
PART = 352
SPART = 176
NS = 2
NC = NX // NS
CH = NS * CAP
SH = 256
VMEM_LIMIT = 60 * 1024 * 1024


SEND = (0, 1, 7, 2, 6, 3, 5, 4)
PLAN = (
    "A0 A1 A7 O",
    "W1 N0 B0 A2",
    "A6 N1 B1 W2",
    "N7 B7 R0 N2",
    "B2 W3 A3 A5",
    "R1 N6 B6 A4",
    "R2 N3 B3 R6",
    "N5 B5 R3 C0",
    "N4 B4 R5 C1",
    "R4 R7 C2 C6",
    "S0 C3 C5 S1",
    "F0 C4 C7 F1",
    "G0 G1 G2 G6",
    "G3 G5 G4 G7",
)


def kernel(
    tok, gain, idst, gatet, shin, shout, win_hbm, wout_hbm, out,
    xall, win, wout, wsin, wsout, code, gm, oh, og, snd, rx, xn, sa, sibin, po, pn, sn, nbrin, ret, back,
    acc, fs, fin, ssa, ssin, spo, spn, sb, shr,
    ld_sem, tok_s, tok_r, tf_s, tf_r, wz_s, wz_r, wy_s, wy_r, dp_s, dp_r, nb_s, nb_r, sq_s, sq_r,
    ra_s, ra_r, rb_s, rb_r, bk_s, bk_r, xs_s, xs_r, sr_s, sr_r, fn_s, fn_r,
):
    gx = lax.axis_index("gx")
    gy = lax.axis_index("gy")
    j, q = gy // 4, gy % 4
    ylo, z = gx // 8, gx % 8
    sib = gy + 1 - 2 * (gy % 2)
    nbr = gy + 2 - 4 * ((gy // 2) % 2)
    qs, qn = sib % 4, nbr % 4
    qsn = (qs + 2) % 4
    ypart = (gx + 8) % NX

    def peer(r):
        return (gy + r) % NY

    def remote(src, dst, send, recv, tx, ty):
        return pltpu.make_async_remote_copy(
            src_ref=src, dst_ref=dst, send_sem=send, recv_sem=recv,
            device_id=(tx, ty), device_id_type=MESH,
        )

    def shift(k, u):
        return 8 * u + k

    def loads():
        for i in range(16):
            p = (i % 4) * 4 + i // 4
            yield pltpu.make_async_copy(
                win_hbm.at[:, pl.ds(i * B, B)], win.at[:, pl.ds(p * B, B)], ld_sem.at[0, i]
            )
            yield pltpu.make_async_copy(
                wout_hbm.at[:, pl.ds(i * B, B)], wout.at[i % 4, :, pl.ds((i // 4) * B, B)], ld_sem.at[1, i]
            )

    for copy in loads():
        copy.start()

    barrier = pltpu.get_barrier_semaphore()
    for r in range(1, NX):
        pl.semaphore_signal(barrier, inc=1, device_id=((gx + r) % NX, gy), device_id_type=MESH)
    for r in range(1, 8):
        pl.semaphore_signal(barrier, inc=1, device_id=(gx, peer(2 * r)), device_id_type=MESH)
    pl.semaphore_signal(barrier, inc=1, device_id=(gx, sib), device_id_type=MESH)

    expert = 4 * lax.broadcasted_iota(jnp.int32, (NX, TOK), 0) + j
    named = jnp.zeros((NX, TOK), F32)
    weight = jnp.zeros((NX, TOK), F32)
    for k in range(TOPK):
        hit = idst[k : k + 1, :] == expert
        named = jnp.where(hit, 1.0, named)
        weight = jnp.where(hit, gatet[k : k + 1, :], weight)
    before = (
        lax.broadcasted_iota(jnp.int32, (TOK, TOK), 0) < lax.broadcasted_iota(jnp.int32, (TOK, TOK), 1)
    )
    count = jnp.dot(
        named.astype(BF16), jnp.where(before, 1.0, 0.0).astype(BF16), preferred_element_type=F32
    )
    code[...] = jnp.where(named > 0.0, count, -1.0)
    gm[...] = weight
    slot = lax.broadcasted_iota(jnp.int32, (CAP, TOK), 0).astype(F32)

    for k in range(NC):
        for u in range(NS):
            m = (gx + shift(k, u)) % NX
            hit = slot == code[pl.ds(m, 1), :]
            at = pl.ds((NS * k + u) * CAP, CAP)
            oh[at, :] = jnp.where(hit, 1.0, 0.0).astype(BF16)
            og[at, :] = jnp.where(hit, gm[pl.ds(m, 1), :], 0.0).astype(BF16)

    pl.semaphore_wait(barrier, NX - 1 + 8)

    def tok_at(owner):
        return xall.at[owner % 4, :, pl.ds(pl.multiple_of((owner // 4) * B, B), B)]

    def tok_send(r):
        return remote(tok, tok_at(gy), tok_s.at[r], tok_r.at[r], gx, peer(2 * r))

    def tok_recv(r):
        place = tok_at(peer(16 - 2 * r))
        return remote(place, place, tok_s.at[r], tok_r.at[r], gx, sib)

    def tok_forward(r):
        place = tok_at(peer(16 - 2 * r))
        return remote(place, place, tf_s.at[r], tf_r.at[r], gx, sib)

    def tok_forwarded(r):
        place = tok_at((sib + 16 - 2 * r) % NY)
        return remote(place, place, tf_s.at[r], tf_r.at[r], gx, sib)

    tok_own = remote(tok, tok_at(gy), tf_s.at[0], tf_r.at[0], gx, sib)
    for r in (2, 4, 6):
        tok_send(r).start()

    def block_z(e):
        if e == 0:
            return z
        step = (e + 1) // 2
        return (z + 8 - step) % 8 if e % 2 else (z + step) % 8

    def w_at(owner):
        place = (owner % 4) * 4 + owner // 4
        return (
            wsin.at[:, :, pl.ds(pl.multiple_of(place * B, B), B)],
            wsout.at[owner % 4, :, pl.ds(pl.multiple_of((owner // 4) * B, B), B)],
        )

    def w_source(e):
        return (shin, shout) if e == 0 else w_at(ylo * 8 + block_z(e))

    def w_ring(e):
        origin = 0 if e <= 2 else e - 2
        target = ylo * 8 + ((z + 1) % 8 if e % 2 else (z + 7) % 8)
        to = w_at(ylo * 8 + block_z(origin))
        return [
            remote(w_source(origin)[t], to[t], wz_s.at[t, e], wz_r.at[t, e], target, gy) for t in range(2)
        ]

    def w_ring_recv(e):
        place = w_at(ylo * 8 + block_z(e))
        return [remote(place[t], place[t], wz_s.at[t, e], wz_r.at[t, e], ypart, gy) for t in range(2)]

    def w_cross(e):
        to = w_at(ylo * 8 + block_z(e))
        return [remote(w_source(e)[t], to[t], wy_s.at[t, e], wy_r.at[t, e], ypart, gy) for t in range(2)]

    def w_cross_recv(e):
        place = w_at((1 - ylo) * 8 + block_z(e))
        return [remote(place[t], place[t], wy_s.at[t, e], wy_r.at[t, e], ypart, gy) for t in range(2)]

    def start(copies):
        for copy in copies:
            copy.start()

    def arrived(copies):
        for copy in copies:
            copy.wait_recv()

    start(w_ring(1))
    start(w_ring(2))
    tok_own.start()
    for r in (1, 3, 5, 7):
        tok_send(r).start()
    start(w_cross(0))

    xall[q, :, pl.ds(pl.multiple_of(j * B, B), B)] = tok[...]
    wsin[:, :, pl.ds(pl.multiple_of(((gx % 4) * 4 + gx // 4) * B, B), B)] = shin[...]
    wsout[gx % 4, :, pl.ds(pl.multiple_of((gx // 4) * B, B), B)] = shout[...]

    def slots_of(k, u):
        return pl.ds((NS * k + u) * CAP, CAP)

    def chunk_of(k):
        return pl.ds(k * CH, CH)

    def dp(k, u):
        return remote(
            snd.at[slots_of(k, u), :], rx.at[q, slots_of(k, u), :],
            dp_s.at[NS * k + u], dp_r.at[NS * k + u], (gx + shift(k, u)) % NX, gy,
        )

    for e in (1, 2):
        arrived(w_ring_recv(e))
        start(w_ring(e + 2))
    for r in (2, 4, 6):
        tok_recv(r).wait_recv()

    for k in SEND:
        picked = jnp.dot(oh[chunk_of(k), :], xall[q], preferred_element_type=F32)
        snd[chunk_of(k), :] = picked.astype(BF16)
        for u in range(NS):
            if shift(k, u):
                dp(k, u).start()
            else:
                pltpu.make_async_copy(
                    snd.at[slots_of(k, u), :], rx.at[q, slots_of(k, u), :], dp_r.at[NS * k + u]
                ).start()
    for e in (1, 2):
        start(w_cross(e))

    def to_nbr(k):
        place = rx.at[q, chunk_of(k), :]
        return remote(place, place, nb_s.at[k], nb_r.at[k], gx, nbr)

    def from_nbr(k):
        place = rx.at[qn, chunk_of(k), :]
        return remote(place, place, nb_s.at[k], nb_r.at[k], gx, nbr)

    def to_sib(t, k):
        place = rx.at[q if t == 0 else qn, chunk_of(k), :]
        return remote(place, place, sq_s.at[t, k], sq_r.at[t, k], gx, sib)

    def from_sib(t, k):
        place = rx.at[qs if t == 0 else qsn, chunk_of(k), :]
        return remote(place, place, sq_s.at[t, k], sq_r.at[t, k], gx, sib)

    def stage_a(k):
        for u in range(NS):
            place = rx.at[q, slots_of(k, u), :]
            remote(place, place, dp_s.at[NS * k + u], dp_r.at[NS * k + u], gx, sib).wait_recv()
        to_nbr(k).start()
        to_sib(0, k).start()

    def stage_a2(k):
        from_nbr(k).wait_recv()
        to_sib(1, k).start()

    def ra(k):
        return remote(sa.at[k], sibin.at[k], ra_s.at[k], ra_r.at[k], gx, sib)

    def rb(k):
        return remote(sn.at[k], nbrin.at[k], rb_s.at[k], rb_r.at[k], gx, nbr)

    def bk(k, u):
        return remote(
            ret.at[slots_of(k, u), :], back.at[slots_of(k, u), :],
            bk_s.at[NS * k + u], bk_r.at[NS * k + u], (gx + NX - shift(k, u)) % NX, gy,
        )

    def dot_nt(a, b):
        return lax.dot_general(a, b, (((1,), (1,)), ((), ())), preferred_element_type=F32)

    def normalise(source, rows, size):
        total = jnp.zeros((size, B), F32)
        for c in range(4):
            for b in range(4):
                value = source[c, rows, b * B : (b + 1) * B].astype(F32)
                total = total + value * value
        inverse = lax.rsqrt(jnp.sum(total, axis=1, keepdims=True) * (1.0 / D) + EPSILON)
        for c in range(4):
            for b in range(4):
                value = source[c, rows, b * B : (b + 1) * B].astype(F32)
                scaled = value * inverse * gain[4 * b + c : 4 * b + c + 1, :]
                xn[:size, c * Q + b * B : c * Q + (b + 1) * B] = scaled.astype(BF16)

    def stage_b(k):
        from_sib(0, k).wait_recv()
        from_sib(1, k).wait_recv()
        normalise(rx, chunk_of(k), CH)
        gate, up = dot_nt(xn[:CH, :], win[:PART, :]), dot_nt(xn[:CH, :], win[PART:, :])
        hidden = (jax.nn.silu(gate) * up).astype(BF16)
        sa[k, 0] = jnp.dot(hidden, wout[qs], preferred_element_type=F32).astype(BF16)
        sa[k, 1] = jnp.dot(hidden, wout[qsn], preferred_element_type=F32).astype(BF16)
        ra(k).start()
        pn[k] = jnp.dot(hidden, wout[qn], preferred_element_type=F32)
        po[k] = jnp.dot(hidden, wout[q], preferred_element_type=F32)

    def stage_rb(k):
        remote(sa.at[k], sibin.at[k], ra_s.at[k], ra_r.at[k], gx, sib).wait_recv()
        sn[k] = (pn[k] + sibin[k, 1].astype(F32)).astype(BF16)
        rb(k).start()
        po[k] = po[k] + sibin[k, 0].astype(F32)

    def stage_c(k):
        remote(sn.at[k], nbrin.at[k], rb_s.at[k], rb_r.at[k], gx, nbr).wait_recv()
        ret[chunk_of(k), :] = (po[k] + nbrin[k].astype(F32)).astype(BF16)
        for u in range(NS):
            if shift(k, u):
                bk(k, u).start()
            else:
                pltpu.make_async_copy(
                    ret.at[slots_of(k, u), :], back.at[slots_of(k, u), :], bk_r.at[NS * k + u]
                ).start()

    def ring(n):
        if n < 3:
            for e in (2 * n + 1, 2 * n + 2):
                arrived(w_ring_recv(e))
                if e + 2 < 8:
                    start(w_ring(e + 2))
            for e in (2 * n + 1, 2 * n + 2):
                start(w_cross(e))
        else:
            arrived(w_ring_recv(7))
            start(w_cross(7))

    def others():
        for r in (2, 4, 6):
            tok_forward(r).start()
        for r in (1, 3, 5, 7):
            tok_recv(r).wait_recv()
            tok_forward(r).start()

    def rows_of(c):
        return pl.ds(pl.multiple_of(c * SH, SH), SH)

    def xs(c):
        return remote(ssa.at[c], ssin.at[c], xs_s.at[c], xs_r.at[c], gx, sib)

    def sr(c, r):
        target = peer(2 * r)
        return remote(
            sb.at[r % 2, rows_of(c), pl.ds(pl.multiple_of((target // 4) * B, B), B)], shr.at[r, rows_of(c), :],
            sr_s.at[c, r], sr_r.at[c, r], gx, target,
        )

    def shared(c):
        if c == 0:
            for r in range(8):
                tok_forwarded(r).wait_recv()
            for e in range(8):
                arrived(w_cross_recv(e))
        rows = rows_of(c)
        normalise(xall, rows, SH)
        gate, up = dot_nt(xn[...], wsin[0]), dot_nt(xn[...], wsin[1])
        hidden = (jax.nn.silu(gate) * up).astype(BF16)
        ssa[c, 0] = jnp.dot(hidden, wsout[qs], preferred_element_type=F32).astype(BF16)
        ssa[c, 1] = jnp.dot(hidden, wsout[qsn], preferred_element_type=F32).astype(BF16)
        xs(c).start()
        spo[rows, :] = jnp.dot(hidden, wsout[q], preferred_element_type=F32)
        spn[rows, :] = jnp.dot(hidden, wsout[qn], preferred_element_type=F32)

    def fold(c):
        rows = rows_of(c)
        xs(c).wait_recv()
        own = spo[rows, :] + ssin[c, 0].astype(F32)
        spo[rows, :] = own
        sb[0, rows, :] = own.astype(BF16)
        sb[1, rows, :] = (spn[rows, :] + ssin[c, 1].astype(F32)).astype(BF16)
        for r in range(1, 8):
            sr(c, r).start()

    summed = []

    def combine(k):
        for u in range(NS):
            bk(k, u).wait_recv()
        rows = chunk_of(k)
        part = lax.dot_general(
            og[rows, :], back[rows, :], (((0,), (0,)), ((), ())), preferred_element_type=F32
        )
        acc[...] = acc[...] + part if summed else part
        summed.append(k)

    steps = {
        "A": stage_a, "N": stage_a2, "B": stage_b, "R": stage_rb, "C": stage_c, "G": combine,
        "S": shared, "F": fold, "W": ring,
    }
    loaded = False
    for step in " ".join(PLAN).split():
        if step == "O":
            others()
            continue
        if step[0] == "B" and not loaded:
            for copy in loads():
                copy.wait()
            loaded = True
        steps[step[0]](int(step[1:]))

    def fn(t):
        return remote(fs.at[t], fin.at[t], fn_s.at[t], fn_r.at[t], gx, peer(4 * t))

    for t in range(1, 4):
        at = pl.multiple_of(((j + t) % 4) * B, B)
        fs[t] = acc[:, pl.ds(at, B)].astype(BF16)
        fn(t).start()
    mine = pl.ds(pl.multiple_of(j * B, B), B)
    total = acc[:, mine] + spo[:, mine]
    for r in range(1, 8):
        for c in range(2):
            sr(c, r).wait_recv()
        total = total + shr[r].astype(F32)
    for t in range(1, 4):
        fn(t).wait_recv()
        total = total + fin[t].astype(F32)
    out[...] = total.astype(BF16)

    tok_own.wait_send()
    for r in range(1, 8):
        tok_send(r).wait_send()
        tok_forward(r).wait_send()
        for c in range(2):
            sr(c, r).wait_send()
        for copy in w_ring(r):
            copy.wait_send()
    for e in range(8):
        for copy in w_cross(e):
            copy.wait_send()
    for c in range(2):
        xs(c).wait_send()
    for t in range(1, 4):
        fn(t).wait_send()

    for k in range(NC):
        to_nbr(k).wait_send()
        to_sib(0, k).wait_send()
        to_sib(1, k).wait_send()
        ra(k).wait_send()
        rb(k).wait_send()
        for u in range(NS):
            if shift(k, u):
                dp(k, u).wait_send()
                bk(k, u).wait_send()


def on_device(tokens, norm_gain, expert_ids, gate_weights, shared_in, shared_out, expert_in, expert_out):
    dma = pltpu.SemaphoreType.DMA
    vmem = pl.BlockSpec(memory_space=pltpu.VMEM)
    anywhere = pl.BlockSpec(memory_space=pl.ANY)
    return pl.pallas_call(
        kernel,
        out_shape=jax.ShapeDtypeStruct((TOK, B), BF16),
        in_specs=[vmem] * 6 + [anywhere] * 2,
        out_specs=vmem,
        scratch_shapes=[
            pltpu.VMEM((4, TOK, Q), BF16),
            pltpu.VMEM((2 * PART, D), BF16),
            pltpu.VMEM((4, PART, Q), BF16),
            pltpu.VMEM((2, SPART, D), BF16),
            pltpu.VMEM((4, SPART, Q), BF16),
            pltpu.VMEM((NX, TOK), F32),
            pltpu.VMEM((NX, TOK), F32),
            pltpu.VMEM((NX * CAP, TOK), BF16),
            pltpu.VMEM((NX * CAP, TOK), BF16),
            pltpu.VMEM((NX * CAP, Q), BF16),
            pltpu.VMEM((4, NX * CAP, Q), BF16),
            pltpu.VMEM((SH, D), BF16),
            pltpu.VMEM((NC, 2, CH, Q), BF16),
            pltpu.VMEM((NC, 2, CH, Q), BF16),
            pltpu.VMEM((NC, CH, Q), F32),
            pltpu.VMEM((NC, CH, Q), F32),
            pltpu.VMEM((NC, CH, Q), BF16),
            pltpu.VMEM((NC, CH, Q), BF16),
            pltpu.VMEM((NX * CAP, Q), BF16),
            pltpu.VMEM((NX * CAP, Q), BF16),
            pltpu.VMEM((TOK, Q), F32),
            pltpu.VMEM((4, TOK, B), BF16),
            pltpu.VMEM((4, TOK, B), BF16),
            pltpu.VMEM((2, 2, SH, Q), BF16),
            pltpu.VMEM((2, 2, SH, Q), BF16),
            pltpu.VMEM((TOK, Q), F32),
            pltpu.VMEM((TOK, Q), F32),
            pltpu.VMEM((2, TOK, Q), BF16),
            pltpu.VMEM((8, TOK, B), BF16),
            dma((2, 16)),
            dma((8,)), dma((8,)),
            dma((8,)), dma((8,)),
            dma((2, 8)), dma((2, 8)),
            dma((2, 8)), dma((2, 8)),
            dma((16,)), dma((16,)),
            dma((NC,)), dma((NC,)),
            dma((2, NC)), dma((2, NC)),
            dma((NC,)), dma((NC,)),
            dma((NC,)), dma((NC,)),
            dma((16,)), dma((16,)),
            dma((2,)), dma((2,)),
            dma((2, 8)), dma((2, 8)),
            dma((4,)), dma((4,)),
        ],
        compiler_params=pltpu.CompilerParams(
            collective_id=0, has_side_effects=True, vmem_limit_bytes=VMEM_LIMIT
        ),
    )(
        tokens, norm_gain.reshape(D // B, B), expert_ids.T, gate_weights.T,
        jnp.swapaxes(shared_in, 1, 2), shared_out,
        expert_in.reshape(D, 2 * PART).T, expert_out.reshape(PART, D),
    )


def solution(mesh):
    in_specs = (
        P("gx", "gy"),
        P(),
        P("gx", None),
        P("gx", None),
        P(None, "gx", "gy"),
        P("gy", "gx"),
        P(("gx", "gy"), None, None),
        P(("gx", "gy"), None, None),
    )
    return jax.shard_map(
        on_device, mesh=mesh, in_specs=in_specs, out_specs=P("gx", "gy"), check_vma=False
    )
```

```python
import jax
import jax.numpy as jnp
from jax import lax
from jax.experimental import pallas as pl
from jax.experimental.pallas import tpu as pltpu
from jax.sharding import PartitionSpec as P

MESH = pl.DeviceIdType.MESH
F32 = jnp.float32
BF16 = jnp.bfloat16
EPSILON = 1e-06

NX = 16
NY = 16
CAP = 64
TOK = 512
D = 2048
B = 128
Q = 512
TOPK = 6
PART = 352
SPART = 176
NS = 2
NC = NX // NS
CH = NS * CAP
SH = 256
VMEM_LIMIT = 60 * 1024 * 1024


SEND = (0, 1, 7, 2, 6, 3, 5, 4)
PLAN = (
    "A0 A1 A7 O",
    "W1 N0 B0 A2",
    "A6 N1 B1 W2",
    "N7 B7 R0 N2",
    "B2 W3 A3 A5",
    "R1 N6 B6 A4",
    "R2 N3 B3 R6",
    "N5 B5 R3 C0",
    "N4 B4 R5 C1",
    "R4 R7 S0 C2",
    "C6 F0 S1 C3",
    "C5 F1 C4 C7",
    "G0 G1 G2 G6",
    "G3 G5 G4 G7",
)


def kernel(
    tok, gain, idst, gatet, shin, shout, win_hbm, wout_hbm, out,
    xall, win, wout, wsin, wsout, code, gm, oh, og, snd, rx, xn, sa, sibin, po, pn, sn, nbrin, ret, back,
    acc, fs, fin, ssa, ssin, spo, spn, sb, shr,
    ld_sem, tok_s, tok_r, tf_s, tf_r, wz_s, wz_r, wy_s, wy_r, dp_s, dp_r, nb_s, nb_r, sq_s, sq_r,
    ra_s, ra_r, rb_s, rb_r, bk_s, bk_r, xs_s, xs_r, sr_s, sr_r, fn_s, fn_r,
):
    gx = lax.axis_index("gx")
    gy = lax.axis_index("gy")
    j, q = gy // 4, gy % 4
    ylo, z = gx // 8, gx % 8
    sib = gy + 1 - 2 * (gy % 2)
    nbr = gy + 2 - 4 * ((gy // 2) % 2)
    qs, qn = sib % 4, nbr % 4
    qsn = (qs + 2) % 4
    ypart = (gx + 8) % NX

    def peer(r):
        return (gy + r) % NY

    def remote(src, dst, send, recv, tx, ty):
        return pltpu.make_async_remote_copy(
            src_ref=src, dst_ref=dst, send_sem=send, recv_sem=recv,
            device_id=(tx, ty), device_id_type=MESH,
        )

    def shift(k, u):
        return 8 * u + k

    def loads():
        for i in range(16):
            p = (i % 4) * 4 + i // 4
            yield pltpu.make_async_copy(
                win_hbm.at[:, pl.ds(i * B, B)], win.at[:, pl.ds(p * B, B)], ld_sem.at[0, i]
            )
            yield pltpu.make_async_copy(
                wout_hbm.at[:, pl.ds(i * B, B)], wout.at[i % 4, :, pl.ds((i // 4) * B, B)], ld_sem.at[1, i]
            )

    for copy in loads():
        copy.start()

    barrier = pltpu.get_barrier_semaphore()
    for r in range(1, NX):
        pl.semaphore_signal(barrier, inc=1, device_id=((gx + r) % NX, gy), device_id_type=MESH)
    for r in range(1, 8):
        pl.semaphore_signal(barrier, inc=1, device_id=(gx, peer(2 * r)), device_id_type=MESH)
    pl.semaphore_signal(barrier, inc=1, device_id=(gx, sib), device_id_type=MESH)

    expert = 4 * lax.broadcasted_iota(jnp.int32, (NX, TOK), 0) + j
    named = jnp.zeros((NX, TOK), F32)
    weight = jnp.zeros((NX, TOK), F32)
    for k in range(TOPK):
        hit = idst[k : k + 1, :] == expert
        named = jnp.where(hit, 1.0, named)
        weight = jnp.where(hit, gatet[k : k + 1, :], weight)
    before = (
        lax.broadcasted_iota(jnp.int32, (TOK, TOK), 0) < lax.broadcasted_iota(jnp.int32, (TOK, TOK), 1)
    )
    count = jnp.dot(
        named.astype(BF16), jnp.where(before, 1.0, 0.0).astype(BF16), preferred_element_type=F32
    )
    code[...] = jnp.where(named > 0.0, count, -1.0)
    gm[...] = weight
    slot = lax.broadcasted_iota(jnp.int32, (CAP, TOK), 0).astype(F32)

    for k in range(NC):
        for u in range(NS):
            m = (gx + shift(k, u)) % NX
            hit = slot == code[pl.ds(m, 1), :]
            at = pl.ds((NS * k + u) * CAP, CAP)
            oh[at, :] = jnp.where(hit, 1.0, 0.0).astype(BF16)
            og[at, :] = jnp.where(hit, gm[pl.ds(m, 1), :], 0.0).astype(BF16)

    pl.semaphore_wait(barrier, NX - 1 + 8)

    def tok_at(owner):
        return xall.at[owner % 4, :, pl.ds(pl.multiple_of((owner // 4) * B, B), B)]

    def tok_send(r):
        return remote(tok, tok_at(gy), tok_s.at[r], tok_r.at[r], gx, peer(2 * r))

    def tok_recv(r):
        place = tok_at(peer(16 - 2 * r))
        return remote(place, place, tok_s.at[r], tok_r.at[r], gx, sib)

    def tok_forward(r):
        place = tok_at(peer(16 - 2 * r))
        return remote(place, place, tf_s.at[r], tf_r.at[r], gx, sib)

    def tok_forwarded(r):
        place = tok_at((sib + 16 - 2 * r) % NY)
        return remote(place, place, tf_s.at[r], tf_r.at[r], gx, sib)

    tok_own = remote(tok, tok_at(gy), tf_s.at[0], tf_r.at[0], gx, sib)
    for r in (2, 4, 6):
        tok_send(r).start()

    def block_z(e):
        if e == 0:
            return z
        step = (e + 1) // 2
        return (z + 8 - step) % 8 if e % 2 else (z + step) % 8

    def w_at(owner):
        place = (owner % 4) * 4 + owner // 4
        return (
            wsin.at[:, :, pl.ds(pl.multiple_of(place * B, B), B)],
            wsout.at[owner % 4, :, pl.ds(pl.multiple_of((owner // 4) * B, B), B)],
        )

    def w_source(e):
        return (shin, shout) if e == 0 else w_at(ylo * 8 + block_z(e))

    def w_ring(e):
        origin = 0 if e <= 2 else e - 2
        target = ylo * 8 + ((z + 1) % 8 if e % 2 else (z + 7) % 8)
        to = w_at(ylo * 8 + block_z(origin))
        return [
            remote(w_source(origin)[t], to[t], wz_s.at[t, e], wz_r.at[t, e], target, gy) for t in range(2)
        ]

    def w_ring_recv(e):
        place = w_at(ylo * 8 + block_z(e))
        return [remote(place[t], place[t], wz_s.at[t, e], wz_r.at[t, e], ypart, gy) for t in range(2)]

    def w_cross(e):
        to = w_at(ylo * 8 + block_z(e))
        return [remote(w_source(e)[t], to[t], wy_s.at[t, e], wy_r.at[t, e], ypart, gy) for t in range(2)]

    def w_cross_recv(e):
        place = w_at((1 - ylo) * 8 + block_z(e))
        return [remote(place[t], place[t], wy_s.at[t, e], wy_r.at[t, e], ypart, gy) for t in range(2)]

    def start(copies):
        for copy in copies:
            copy.start()

    def arrived(copies):
        for copy in copies:
            copy.wait_recv()

    start(w_ring(1))
    start(w_ring(2))

    xall[q, :, pl.ds(pl.multiple_of(j * B, B), B)] = tok[...]
    wsin[:, :, pl.ds(pl.multiple_of(((gx % 4) * 4 + gx // 4) * B, B), B)] = shin[...]
    wsout[gx % 4, :, pl.ds(pl.multiple_of((gx // 4) * B, B), B)] = shout[...]

    def slots_of(k, u):
        return pl.ds((NS * k + u) * CAP, CAP)

    def chunk_of(k):
        return pl.ds(k * CH, CH)

    def dp(k, u):
        return remote(
            snd.at[slots_of(k, u), :], rx.at[q, slots_of(k, u), :],
            dp_s.at[NS * k + u], dp_r.at[NS * k + u], (gx + shift(k, u)) % NX, gy,
        )

    for e in (1, 2):
        arrived(w_ring_recv(e))
        start(w_ring(e + 2))
    for r in (2, 4, 6):
        tok_recv(r).wait_recv()
    tok_own.start()
    for r in (1, 3, 5, 7):
        tok_send(r).start()
    start(w_cross(0))

    for k in SEND:
        picked = jnp.dot(oh[chunk_of(k), :], xall[q], preferred_element_type=F32)
        snd[chunk_of(k), :] = picked.astype(BF16)
        for u in range(NS):
            if shift(k, u):
                dp(k, u).start()
            else:
                pltpu.make_async_copy(
                    snd.at[slots_of(k, u), :], rx.at[q, slots_of(k, u), :], dp_r.at[NS * k + u]
                ).start()
    for e in (1, 2):
        start(w_cross(e))

    def to_nbr(k):
        place = rx.at[q, chunk_of(k), :]
        return remote(place, place, nb_s.at[k], nb_r.at[k], gx, nbr)

    def from_nbr(k):
        place = rx.at[qn, chunk_of(k), :]
        return remote(place, place, nb_s.at[k], nb_r.at[k], gx, nbr)

    def to_sib(t, k):
        place = rx.at[q if t == 0 else qn, chunk_of(k), :]
        return remote(place, place, sq_s.at[t, k], sq_r.at[t, k], gx, sib)

    def from_sib(t, k):
        place = rx.at[qs if t == 0 else qsn, chunk_of(k), :]
        return remote(place, place, sq_s.at[t, k], sq_r.at[t, k], gx, sib)

    def stage_a(k):
        for u in range(NS):
            place = rx.at[q, slots_of(k, u), :]
            remote(place, place, dp_s.at[NS * k + u], dp_r.at[NS * k + u], gx, sib).wait_recv()
        to_nbr(k).start()
        to_sib(0, k).start()

    def stage_a2(k):
        from_nbr(k).wait_recv()
        to_sib(1, k).start()

    def ra(k):
        return remote(sa.at[k], sibin.at[k], ra_s.at[k], ra_r.at[k], gx, sib)

    def rb(k):
        return remote(sn.at[k], nbrin.at[k], rb_s.at[k], rb_r.at[k], gx, nbr)

    def bk(k, u):
        return remote(
            ret.at[slots_of(k, u), :], back.at[slots_of(k, u), :],
            bk_s.at[NS * k + u], bk_r.at[NS * k + u], (gx + NX - shift(k, u)) % NX, gy,
        )

    def dot_nt(a, b):
        return lax.dot_general(a, b, (((1,), (1,)), ((), ())), preferred_element_type=F32)

    def normalise(source, rows, size):
        total = jnp.zeros((size, B), F32)
        for c in range(4):
            for b in range(4):
                value = source[c, rows, b * B : (b + 1) * B].astype(F32)
                total = total + value * value
        inverse = lax.rsqrt(jnp.sum(total, axis=1, keepdims=True) * (1.0 / D) + EPSILON)
        for c in range(4):
            for b in range(4):
                value = source[c, rows, b * B : (b + 1) * B].astype(F32)
                scaled = value * inverse * gain[4 * b + c : 4 * b + c + 1, :]
                xn[:size, c * Q + b * B : c * Q + (b + 1) * B] = scaled.astype(BF16)

    def stage_b(k):
        from_sib(0, k).wait_recv()
        from_sib(1, k).wait_recv()
        normalise(rx, chunk_of(k), CH)
        gate, up = dot_nt(xn[:CH, :], win[:PART, :]), dot_nt(xn[:CH, :], win[PART:, :])
        hidden = (jax.nn.silu(gate) * up).astype(BF16)
        sa[k, 0] = jnp.dot(hidden, wout[qs], preferred_element_type=F32).astype(BF16)
        sa[k, 1] = jnp.dot(hidden, wout[qsn], preferred_element_type=F32).astype(BF16)
        ra(k).start()
        pn[k] = jnp.dot(hidden, wout[qn], preferred_element_type=F32)
        po[k] = jnp.dot(hidden, wout[q], preferred_element_type=F32)

    def stage_rb(k):
        remote(sa.at[k], sibin.at[k], ra_s.at[k], ra_r.at[k], gx, sib).wait_recv()
        sn[k] = (pn[k] + sibin[k, 1].astype(F32)).astype(BF16)
        rb(k).start()
        po[k] = po[k] + sibin[k, 0].astype(F32)

    def stage_c(k):
        remote(sn.at[k], nbrin.at[k], rb_s.at[k], rb_r.at[k], gx, nbr).wait_recv()
        ret[chunk_of(k), :] = (po[k] + nbrin[k].astype(F32)).astype(BF16)
        for u in range(NS):
            if shift(k, u):
                bk(k, u).start()
            else:
                pltpu.make_async_copy(
                    ret.at[slots_of(k, u), :], back.at[slots_of(k, u), :], bk_r.at[NS * k + u]
                ).start()

    def ring(n):
        if n < 3:
            for e in (2 * n + 1, 2 * n + 2):
                arrived(w_ring_recv(e))
                if e + 2 < 8:
                    start(w_ring(e + 2))
            for e in (2 * n + 1, 2 * n + 2):
                start(w_cross(e))
        else:
            arrived(w_ring_recv(7))
            start(w_cross(7))

    def others():
        for r in (2, 4, 6):
            tok_forward(r).start()
        for r in (1, 3, 5, 7):
            tok_recv(r).wait_recv()
            tok_forward(r).start()

    def rows_of(c):
        return pl.ds(pl.multiple_of(c * SH, SH), SH)

    def xs(c):
        return remote(ssa.at[c], ssin.at[c], xs_s.at[c], xs_r.at[c], gx, sib)

    def sr(c, r):
        target = peer(2 * r)
        return remote(
            sb.at[r % 2, rows_of(c), pl.ds(pl.multiple_of((target // 4) * B, B), B)], shr.at[r, rows_of(c), :],
            sr_s.at[c, r], sr_r.at[c, r], gx, target,
        )

    def shared(c):
        if c == 0:
            for r in range(8):
                tok_forwarded(r).wait_recv()
            for e in range(8):
                arrived(w_cross_recv(e))
        rows = rows_of(c)
        normalise(xall, rows, SH)
        gate, up = dot_nt(xn[...], wsin[0]), dot_nt(xn[...], wsin[1])
        hidden = (jax.nn.silu(gate) * up).astype(BF16)
        ssa[c, 0] = jnp.dot(hidden, wsout[qs], preferred_element_type=F32).astype(BF16)
        ssa[c, 1] = jnp.dot(hidden, wsout[qsn], preferred_element_type=F32).astype(BF16)
        xs(c).start()
        spo[rows, :] = jnp.dot(hidden, wsout[q], preferred_element_type=F32)
        spn[rows, :] = jnp.dot(hidden, wsout[qn], preferred_element_type=F32)

    def fold(c):
        rows = rows_of(c)
        xs(c).wait_recv()
        own = spo[rows, :] + ssin[c, 0].astype(F32)
        spo[rows, :] = own
        sb[0, rows, :] = own.astype(BF16)
        sb[1, rows, :] = (spn[rows, :] + ssin[c, 1].astype(F32)).astype(BF16)
        for r in range(1, 8):
            sr(c, r).start()

    summed = []

    def combine(k):
        for u in range(NS):
            bk(k, u).wait_recv()
        rows = chunk_of(k)
        part = lax.dot_general(
            og[rows, :], back[rows, :], (((0,), (0,)), ((), ())), preferred_element_type=F32
        )
        acc[...] = acc[...] + part if summed else part
        summed.append(k)

    steps = {
        "A": stage_a, "N": stage_a2, "B": stage_b, "R": stage_rb, "C": stage_c, "G": combine,
        "S": shared, "F": fold, "W": ring,
    }
    loaded = False
    for step in " ".join(PLAN).split():
        if step == "O":
            others()
            continue
        if step[0] == "B" and not loaded:
            for copy in loads():
                copy.wait()
            loaded = True
        steps[step[0]](int(step[1:]))

    def fn(t):
        return remote(fs.at[t], fin.at[t], fn_s.at[t], fn_r.at[t], gx, peer(4 * t))

    for t in range(1, 4):
        at = pl.multiple_of(((j + t) % 4) * B, B)
        fs[t] = acc[:, pl.ds(at, B)].astype(BF16)
        fn(t).start()
    mine = pl.ds(pl.multiple_of(j * B, B), B)
    total = acc[:, mine] + spo[:, mine]
    for r in range(1, 8):
        for c in range(2):
            sr(c, r).wait_recv()
        total = total + shr[r].astype(F32)
    for t in range(1, 4):
        fn(t).wait_recv()
        total = total + fin[t].astype(F32)
    out[...] = total.astype(BF16)

    tok_own.wait_send()
    for r in range(1, 8):
        tok_send(r).wait_send()
        tok_forward(r).wait_send()
        for c in range(2):
            sr(c, r).wait_send()
        for copy in w_ring(r):
            copy.wait_send()
    for e in range(8):
        for copy in w_cross(e):
            copy.wait_send()
    for c in range(2):
        xs(c).wait_send()
    for t in range(1, 4):
        fn(t).wait_send()

    for k in range(NC):
        to_nbr(k).wait_send()
        to_sib(0, k).wait_send()
        to_sib(1, k).wait_send()
        ra(k).wait_send()
        rb(k).wait_send()
        for u in range(NS):
            if shift(k, u):
                dp(k, u).wait_send()
                bk(k, u).wait_send()


def on_device(tokens, norm_gain, expert_ids, gate_weights, shared_in, shared_out, expert_in, expert_out):
    dma = pltpu.SemaphoreType.DMA
    vmem = pl.BlockSpec(memory_space=pltpu.VMEM)
    anywhere = pl.BlockSpec(memory_space=pl.ANY)
    return pl.pallas_call(
        kernel,
        out_shape=jax.ShapeDtypeStruct((TOK, B), BF16),
        in_specs=[vmem] * 6 + [anywhere] * 2,
        out_specs=vmem,
        scratch_shapes=[
            pltpu.VMEM((4, TOK, Q), BF16),
            pltpu.VMEM((2 * PART, D), BF16),
            pltpu.VMEM((4, PART, Q), BF16),
            pltpu.VMEM((2, SPART, D), BF16),
            pltpu.VMEM((4, SPART, Q), BF16),
            pltpu.VMEM((NX, TOK), F32),
            pltpu.VMEM((NX, TOK), F32),
            pltpu.VMEM((NX * CAP, TOK), BF16),
            pltpu.VMEM((NX * CAP, TOK), BF16),
            pltpu.VMEM((NX * CAP, Q), BF16),
            pltpu.VMEM((4, NX * CAP, Q), BF16),
            pltpu.VMEM((SH, D), BF16),
            pltpu.VMEM((NC, 2, CH, Q), BF16),
            pltpu.VMEM((NC, 2, CH, Q), BF16),
            pltpu.VMEM((NC, CH, Q), F32),
            pltpu.VMEM((NC, CH, Q), F32),
            pltpu.VMEM((NC, CH, Q), BF16),
            pltpu.VMEM((NC, CH, Q), BF16),
            pltpu.VMEM((NX * CAP, Q), BF16),
            pltpu.VMEM((NX * CAP, Q), BF16),
            pltpu.VMEM((TOK, Q), F32),
            pltpu.VMEM((4, TOK, B), BF16),
            pltpu.VMEM((4, TOK, B), BF16),
            pltpu.VMEM((2, 2, SH, Q), BF16),
            pltpu.VMEM((2, 2, SH, Q), BF16),
            pltpu.VMEM((TOK, Q), F32),
            pltpu.VMEM((TOK, Q), F32),
            pltpu.VMEM((2, TOK, Q), BF16),
            pltpu.VMEM((8, TOK, B), BF16),
            dma((2, 16)),
            dma((8,)), dma((8,)),
            dma((8,)), dma((8,)),
            dma((2, 8)), dma((2, 8)),
            dma((2, 8)), dma((2, 8)),
            dma((16,)), dma((16,)),
            dma((NC,)), dma((NC,)),
            dma((2, NC)), dma((2, NC)),
            dma((NC,)), dma((NC,)),
            dma((NC,)), dma((NC,)),
            dma((16,)), dma((16,)),
            dma((2,)), dma((2,)),
            dma((2, 8)), dma((2, 8)),
            dma((4,)), dma((4,)),
        ],
        compiler_params=pltpu.CompilerParams(
            collective_id=0, has_side_effects=True, vmem_limit_bytes=VMEM_LIMIT
        ),
    )(
        tokens, norm_gain.reshape(D // B, B), expert_ids.T, gate_weights.T,
        jnp.swapaxes(shared_in, 1, 2), shared_out,
        expert_in.reshape(D, 2 * PART).T, expert_out.reshape(PART, D),
    )


def solution(mesh):
    in_specs = (
        P("gx", "gy"),
        P(),
        P("gx", None),
        P("gx", None),
        P(None, "gx", "gy"),
        P("gy", "gx"),
        P(("gx", "gy"), None, None),
        P(("gx", "gy"), None, None),
    )
    return jax.shard_map(
        on_device, mesh=mesh, in_specs=in_specs, out_specs=P("gx", "gy"), check_vma=False
    )
```

```python
import jax
import jax.numpy as jnp
from jax import lax
from jax.experimental import pallas as pl
from jax.experimental.pallas import tpu as pltpu
from jax.sharding import PartitionSpec as P

MESH = pl.DeviceIdType.MESH
F32 = jnp.float32
BF16 = jnp.bfloat16
EPSILON = 1e-06

NX = 16
NY = 16
CAP = 64
TOK = 512
D = 2048
B = 128
Q = 512
TOPK = 6
PART = 352
SPART = 176
NS = 2
NC = NX // NS
CH = NS * CAP
SH = 256
VMEM_LIMIT = 60 * 1024 * 1024


SEND = (0, 1, 7, 2, 6, 3, 5, 4)
PLAN = (
    "A0 A1 A7 O",
    "W1 N0 B0 A2",
    "A6 N1 B1 W2",
    "N7 B7 R1 N2",
    "B2 W3 A3 A5",
    "R7 N6 B6 A4",
    "R2 N3 B3 R6",
    "N5 B5 R3 C1",
    "N4 B4 R5 C7",
    "R4 R0 S0 C2",
    "C6 F0 S1 C3",
    "C5 F1 C4 C0",
    "G1 G7 G2 G6",
    "G3 G5 G4 G0",
)


def kernel(
    tok, gain, idst, gatet, shin, shout, win_hbm, wout_hbm, out,
    xall, win, wout, wsin, wsout, code, gm, oh, og, snd, rx, xn, sa, sibin, po, pn, sn, nbrin, ret, back,
    acc, fs, fin, ssa, ssin, spo, spn, sb, shr,
    ld_sem, tok_s, tok_r, tf_s, tf_r, wz_s, wz_r, wy_s, wy_r, dp_s, dp_r, nb_s, nb_r, sq_s, sq_r,
    ra_s, ra_r, rb_s, rb_r, bk_s, bk_r, xs_s, xs_r, sr_s, sr_r, fn_s, fn_r,
):
    gx = lax.axis_index("gx")
    gy = lax.axis_index("gy")
    j, q = gy // 4, gy % 4
    ylo, z = gx // 8, gx % 8
    sib = gy + 1 - 2 * (gy % 2)
    nbr = gy + 2 - 4 * ((gy // 2) % 2)
    qs, qn = sib % 4, nbr % 4
    qsn = (qs + 2) % 4
    ypart = (gx + 8) % NX

    def peer(r):
        return (gy + r) % NY

    def remote(src, dst, send, recv, tx, ty):
        return pltpu.make_async_remote_copy(
            src_ref=src, dst_ref=dst, send_sem=send, recv_sem=recv,
            device_id=(tx, ty), device_id_type=MESH,
        )

    def shift(k, u):
        return 8 * u + k

    def loads():
        for i in range(16):
            p = (i % 4) * 4 + i // 4
            yield pltpu.make_async_copy(
                win_hbm.at[:, pl.ds(i * B, B)], win.at[:, pl.ds(p * B, B)], ld_sem.at[0, i]
            )
            yield pltpu.make_async_copy(
                wout_hbm.at[:, pl.ds(i * B, B)], wout.at[i % 4, :, pl.ds((i // 4) * B, B)], ld_sem.at[1, i]
            )

    for copy in loads():
        copy.start()

    barrier = pltpu.get_barrier_semaphore()
    for r in range(1, NX):
        pl.semaphore_signal(barrier, inc=1, device_id=((gx + r) % NX, gy), device_id_type=MESH)
    for r in range(1, 8):
        pl.semaphore_signal(barrier, inc=1, device_id=(gx, peer(2 * r)), device_id_type=MESH)
    pl.semaphore_signal(barrier, inc=1, device_id=(gx, sib), device_id_type=MESH)

    expert = 4 * lax.broadcasted_iota(jnp.int32, (NX, TOK), 0) + j
    named = jnp.zeros((NX, TOK), F32)
    weight = jnp.zeros((NX, TOK), F32)
    for k in range(TOPK):
        hit = idst[k : k + 1, :] == expert
        named = jnp.where(hit, 1.0, named)
        weight = jnp.where(hit, gatet[k : k + 1, :], weight)
    before = (
        lax.broadcasted_iota(jnp.int32, (TOK, TOK), 0) < lax.broadcasted_iota(jnp.int32, (TOK, TOK), 1)
    )
    count = jnp.dot(
        named.astype(BF16), jnp.where(before, 1.0, 0.0).astype(BF16), preferred_element_type=F32
    )
    code[...] = jnp.where(named > 0.0, count, -1.0)
    gm[...] = weight
    slot = lax.broadcasted_iota(jnp.int32, (CAP, TOK), 0).astype(F32)

    for k in range(NC):
        for u in range(NS):
            m = (gx + shift(k, u)) % NX
            hit = slot == code[pl.ds(m, 1), :]
            at = pl.ds((NS * k + u) * CAP, CAP)
            oh[at, :] = jnp.where(hit, 1.0, 0.0).astype(BF16)
            og[at, :] = jnp.where(hit, gm[pl.ds(m, 1), :], 0.0).astype(BF16)

    pl.semaphore_wait(barrier, NX - 1 + 8)

    def tok_at(owner):
        return xall.at[owner % 4, :, pl.ds(pl.multiple_of((owner // 4) * B, B), B)]

    def tok_send(r):
        return remote(tok, tok_at(gy), tok_s.at[r], tok_r.at[r], gx, peer(2 * r))

    def tok_recv(r):
        place = tok_at(peer(16 - 2 * r))
        return remote(place, place, tok_s.at[r], tok_r.at[r], gx, sib)

    def tok_forward(r):
        place = tok_at(peer(16 - 2 * r))
        return remote(place, place, tf_s.at[r], tf_r.at[r], gx, sib)

    def tok_forwarded(r):
        place = tok_at((sib + 16 - 2 * r) % NY)
        return remote(place, place, tf_s.at[r], tf_r.at[r], gx, sib)

    tok_own = remote(tok, tok_at(gy), tf_s.at[0], tf_r.at[0], gx, sib)
    for r in (2, 4, 6):
        tok_send(r).start()

    def block_z(e):
        if e == 0:
            return z
        step = (e + 1) // 2
        return (z + 8 - step) % 8 if e % 2 else (z + step) % 8

    def w_at(owner):
        place = (owner % 4) * 4 + owner // 4
        return (
            wsin.at[:, :, pl.ds(pl.multiple_of(place * B, B), B)],
            wsout.at[owner % 4, :, pl.ds(pl.multiple_of((owner // 4) * B, B), B)],
        )

    def w_source(e):
        return (shin, shout) if e == 0 else w_at(ylo * 8 + block_z(e))

    def w_ring(e):
        origin = 0 if e <= 2 else e - 2
        target = ylo * 8 + ((z + 1) % 8 if e % 2 else (z + 7) % 8)
        to = w_at(ylo * 8 + block_z(origin))
        return [
            remote(w_source(origin)[t], to[t], wz_s.at[t, e], wz_r.at[t, e], target, gy) for t in range(2)
        ]

    def w_ring_recv(e):
        place = w_at(ylo * 8 + block_z(e))
        return [remote(place[t], place[t], wz_s.at[t, e], wz_r.at[t, e], ypart, gy) for t in range(2)]

    def w_cross(e):
        to = w_at(ylo * 8 + block_z(e))
        return [remote(w_source(e)[t], to[t], wy_s.at[t, e], wy_r.at[t, e], ypart, gy) for t in range(2)]

    def w_cross_recv(e):
        place = w_at((1 - ylo) * 8 + block_z(e))
        return [remote(place[t], place[t], wy_s.at[t, e], wy_r.at[t, e], ypart, gy) for t in range(2)]

    def start(copies):
        for copy in copies:
            copy.start()

    def arrived(copies):
        for copy in copies:
            copy.wait_recv()

    start(w_ring(1))
    start(w_ring(2))

    xall[q, :, pl.ds(pl.multiple_of(j * B, B), B)] = tok[...]
    wsin[:, :, pl.ds(pl.multiple_of(((gx % 4) * 4 + gx // 4) * B, B), B)] = shin[...]
    wsout[gx % 4, :, pl.ds(pl.multiple_of((gx // 4) * B, B), B)] = shout[...]

    def slots_of(k, u):
        return pl.ds((NS * k + u) * CAP, CAP)

    def chunk_of(k):
        return pl.ds(k * CH, CH)

    def dp(k, u):
        return remote(
            snd.at[slots_of(k, u), :], rx.at[q, slots_of(k, u), :],
            dp_s.at[NS * k + u], dp_r.at[NS * k + u], (gx + shift(k, u)) % NX, gy,
        )

    for e in (1, 2):
        arrived(w_ring_recv(e))
        start(w_ring(e + 2))
    for r in (2, 4, 6):
        tok_recv(r).wait_recv()
    tok_own.start()
    for r in (1, 3, 5, 7):
        tok_send(r).start()
    start(w_cross(0))

    for k in SEND:
        picked = jnp.dot(oh[chunk_of(k), :], xall[q], preferred_element_type=F32)
        snd[chunk_of(k), :] = picked.astype(BF16)
        for u in range(NS):
            if shift(k, u):
                dp(k, u).start()
            else:
                pltpu.make_async_copy(
                    snd.at[slots_of(k, u), :], rx.at[q, slots_of(k, u), :], dp_r.at[NS * k + u]
                ).start()
    for e in (1, 2):
        start(w_cross(e))

    def to_nbr(k):
        place = rx.at[q, chunk_of(k), :]
        return remote(place, place, nb_s.at[k], nb_r.at[k], gx, nbr)

    def from_nbr(k):
        place = rx.at[qn, chunk_of(k), :]
        return remote(place, place, nb_s.at[k], nb_r.at[k], gx, nbr)

    def to_sib(t, k):
        place = rx.at[q if t == 0 else qn, chunk_of(k), :]
        return remote(place, place, sq_s.at[t, k], sq_r.at[t, k], gx, sib)

    def from_sib(t, k):
        place = rx.at[qs if t == 0 else qsn, chunk_of(k), :]
        return remote(place, place, sq_s.at[t, k], sq_r.at[t, k], gx, sib)

    def stage_a(k):
        for u in range(NS):
            place = rx.at[q, slots_of(k, u), :]
            remote(place, place, dp_s.at[NS * k + u], dp_r.at[NS * k + u], gx, sib).wait_recv()
        to_nbr(k).start()
        to_sib(0, k).start()

    def stage_a2(k):
        from_nbr(k).wait_recv()
        to_sib(1, k).start()

    def ra(k):
        return remote(sa.at[k], sibin.at[k], ra_s.at[k], ra_r.at[k], gx, sib)

    def rb(k):
        return remote(sn.at[k], nbrin.at[k], rb_s.at[k], rb_r.at[k], gx, nbr)

    def bk(k, u):
        return remote(
            ret.at[slots_of(k, u), :], back.at[slots_of(k, u), :],
            bk_s.at[NS * k + u], bk_r.at[NS * k + u], (gx + NX - shift(k, u)) % NX, gy,
        )

    def dot_nt(a, b):
        return lax.dot_general(a, b, (((1,), (1,)), ((), ())), preferred_element_type=F32)

    def normalise(source, rows, size):
        total = jnp.zeros((size, B), F32)
        for c in range(4):
            for b in range(4):
                value = source[c, rows, b * B : (b + 1) * B].astype(F32)
                total = total + value * value
        inverse = lax.rsqrt(jnp.sum(total, axis=1, keepdims=True) * (1.0 / D) + EPSILON)
        for c in range(4):
            for b in range(4):
                value = source[c, rows, b * B : (b + 1) * B].astype(F32)
                scaled = value * inverse * gain[4 * b + c : 4 * b + c + 1, :]
                xn[:size, c * Q + b * B : c * Q + (b + 1) * B] = scaled.astype(BF16)

    def stage_b(k):
        from_sib(0, k).wait_recv()
        from_sib(1, k).wait_recv()
        normalise(rx, chunk_of(k), CH)
        gate, up = dot_nt(xn[:CH, :], win[:PART, :]), dot_nt(xn[:CH, :], win[PART:, :])
        hidden = (jax.nn.silu(gate) * up).astype(BF16)
        sa[k, 0] = jnp.dot(hidden, wout[qs], preferred_element_type=F32).astype(BF16)
        sa[k, 1] = jnp.dot(hidden, wout[qsn], preferred_element_type=F32).astype(BF16)
        ra(k).start()
        pn[k] = jnp.dot(hidden, wout[qn], preferred_element_type=F32)
        po[k] = jnp.dot(hidden, wout[q], preferred_element_type=F32)

    def stage_rb(k):
        remote(sa.at[k], sibin.at[k], ra_s.at[k], ra_r.at[k], gx, sib).wait_recv()
        sn[k] = (pn[k] + sibin[k, 1].astype(F32)).astype(BF16)
        rb(k).start()
        po[k] = po[k] + sibin[k, 0].astype(F32)

    def stage_c(k):
        remote(sn.at[k], nbrin.at[k], rb_s.at[k], rb_r.at[k], gx, nbr).wait_recv()
        ret[chunk_of(k), :] = (po[k] + nbrin[k].astype(F32)).astype(BF16)
        for u in range(NS):
            if shift(k, u):
                bk(k, u).start()
            else:
                pltpu.make_async_copy(
                    ret.at[slots_of(k, u), :], back.at[slots_of(k, u), :], bk_r.at[NS * k + u]
                ).start()

    def ring(n):
        if n < 3:
            for e in (2 * n + 1, 2 * n + 2):
                arrived(w_ring_recv(e))
                if e + 2 < 8:
                    start(w_ring(e + 2))
            for e in (2 * n + 1, 2 * n + 2):
                start(w_cross(e))
        else:
            arrived(w_ring_recv(7))
            start(w_cross(7))

    def others():
        for r in (2, 4, 6):
            tok_forward(r).start()
        for r in (1, 3, 5, 7):
            tok_recv(r).wait_recv()
            tok_forward(r).start()

    def rows_of(c):
        return pl.ds(pl.multiple_of(c * SH, SH), SH)

    def xs(c):
        return remote(ssa.at[c], ssin.at[c], xs_s.at[c], xs_r.at[c], gx, sib)

    def sr(c, r):
        target = peer(2 * r)
        return remote(
            sb.at[r % 2, rows_of(c), pl.ds(pl.multiple_of((target // 4) * B, B), B)], shr.at[r, rows_of(c), :],
            sr_s.at[c, r], sr_r.at[c, r], gx, target,
        )

    def shared(c):
        if c == 0:
            for r in range(8):
                tok_forwarded(r).wait_recv()
            for e in range(8):
                arrived(w_cross_recv(e))
        rows = rows_of(c)
        normalise(xall, rows, SH)
        gate, up = dot_nt(xn[...], wsin[0]), dot_nt(xn[...], wsin[1])
        hidden = (jax.nn.silu(gate) * up).astype(BF16)
        ssa[c, 0] = jnp.dot(hidden, wsout[qs], preferred_element_type=F32).astype(BF16)
        ssa[c, 1] = jnp.dot(hidden, wsout[qsn], preferred_element_type=F32).astype(BF16)
        xs(c).start()
        spo[rows, :] = jnp.dot(hidden, wsout[q], preferred_element_type=F32)
        spn[rows, :] = jnp.dot(hidden, wsout[qn], preferred_element_type=F32)

    def fold(c):
        rows = rows_of(c)
        xs(c).wait_recv()
        own = spo[rows, :] + ssin[c, 0].astype(F32)
        spo[rows, :] = own
        sb[0, rows, :] = own.astype(BF16)
        sb[1, rows, :] = (spn[rows, :] + ssin[c, 1].astype(F32)).astype(BF16)
        for r in range(1, 8):
            sr(c, r).start()

    summed = []

    def combine(k):
        for u in range(NS):
            bk(k, u).wait_recv()
        rows = chunk_of(k)
        part = lax.dot_general(
            og[rows, :], back[rows, :], (((0,), (0,)), ((), ())), preferred_element_type=F32
        )
        acc[...] = acc[...] + part if summed else part
        summed.append(k)

    steps = {
        "A": stage_a, "N": stage_a2, "B": stage_b, "R": stage_rb, "C": stage_c, "G": combine,
        "S": shared, "F": fold, "W": ring,
    }
    loaded = False
    for step in " ".join(PLAN).split():
        if step == "O":
            others()
            continue
        if step[0] == "B" and not loaded:
            for copy in loads():
                copy.wait()
            loaded = True
        steps[step[0]](int(step[1:]))

    def fn(t):
        return remote(fs.at[t], fin.at[t], fn_s.at[t], fn_r.at[t], gx, peer(4 * t))

    for t in range(1, 4):
        at = pl.multiple_of(((j + t) % 4) * B, B)
        fs[t] = acc[:, pl.ds(at, B)].astype(BF16)
        fn(t).start()
    mine = pl.ds(pl.multiple_of(j * B, B), B)
    total = acc[:, mine] + spo[:, mine]
    for r in range(1, 8):
        for c in range(2):
            sr(c, r).wait_recv()
        total = total + shr[r].astype(F32)
    for t in range(1, 4):
        fn(t).wait_recv()
        total = total + fin[t].astype(F32)
    out[...] = total.astype(BF16)

    tok_own.wait_send()
    for r in range(1, 8):
        tok_send(r).wait_send()
        tok_forward(r).wait_send()
        for c in range(2):
            sr(c, r).wait_send()
        for copy in w_ring(r):
            copy.wait_send()
    for e in range(8):
        for copy in w_cross(e):
            copy.wait_send()
    for c in range(2):
        xs(c).wait_send()
    for t in range(1, 4):
        fn(t).wait_send()

    for k in range(NC):
        to_nbr(k).wait_send()
        to_sib(0, k).wait_send()
        to_sib(1, k).wait_send()
        ra(k).wait_send()
        rb(k).wait_send()
        for u in range(NS):
            if shift(k, u):
                dp(k, u).wait_send()
                bk(k, u).wait_send()


def on_device(tokens, norm_gain, expert_ids, gate_weights, shared_in, shared_out, expert_in, expert_out):
    dma = pltpu.SemaphoreType.DMA
    vmem = pl.BlockSpec(memory_space=pltpu.VMEM)
    anywhere = pl.BlockSpec(memory_space=pl.ANY)
    return pl.pallas_call(
        kernel,
        out_shape=jax.ShapeDtypeStruct((TOK, B), BF16),
        in_specs=[vmem] * 6 + [anywhere] * 2,
        out_specs=vmem,
        scratch_shapes=[
            pltpu.VMEM((4, TOK, Q), BF16),
            pltpu.VMEM((2 * PART, D), BF16),
            pltpu.VMEM((4, PART, Q), BF16),
            pltpu.VMEM((2, SPART, D), BF16),
            pltpu.VMEM((4, SPART, Q), BF16),
            pltpu.VMEM((NX, TOK), F32),
            pltpu.VMEM((NX, TOK), F32),
            pltpu.VMEM((NX * CAP, TOK), BF16),
            pltpu.VMEM((NX * CAP, TOK), BF16),
            pltpu.VMEM((NX * CAP, Q), BF16),
            pltpu.VMEM((4, NX * CAP, Q), BF16),
            pltpu.VMEM((SH, D), BF16),
            pltpu.VMEM((NC, 2, CH, Q), BF16),
            pltpu.VMEM((NC, 2, CH, Q), BF16),
            pltpu.VMEM((NC, CH, Q), F32),
            pltpu.VMEM((NC, CH, Q), F32),
            pltpu.VMEM((NC, CH, Q), BF16),
            pltpu.VMEM((NC, CH, Q), BF16),
            pltpu.VMEM((NX * CAP, Q), BF16),
            pltpu.VMEM((NX * CAP, Q), BF16),
            pltpu.VMEM((TOK, Q), F32),
            pltpu.VMEM((4, TOK, B), BF16),
            pltpu.VMEM((4, TOK, B), BF16),
            pltpu.VMEM((2, 2, SH, Q), BF16),
            pltpu.VMEM((2, 2, SH, Q), BF16),
            pltpu.VMEM((TOK, Q), F32),
            pltpu.VMEM((TOK, Q), F32),
            pltpu.VMEM((2, TOK, Q), BF16),
            pltpu.VMEM((8, TOK, B), BF16),
            dma((2, 16)),
            dma((8,)), dma((8,)),
            dma((8,)), dma((8,)),
            dma((2, 8)), dma((2, 8)),
            dma((2, 8)), dma((2, 8)),
            dma((16,)), dma((16,)),
            dma((NC,)), dma((NC,)),
            dma((2, NC)), dma((2, NC)),
            dma((NC,)), dma((NC,)),
            dma((NC,)), dma((NC,)),
            dma((16,)), dma((16,)),
            dma((2,)), dma((2,)),
            dma((2, 8)), dma((2, 8)),
            dma((4,)), dma((4,)),
        ],
        compiler_params=pltpu.CompilerParams(
            collective_id=0, has_side_effects=True, vmem_limit_bytes=VMEM_LIMIT
        ),
    )(
        tokens, norm_gain.reshape(D // B, B), expert_ids.T, gate_weights.T,
        jnp.swapaxes(shared_in, 1, 2), shared_out,
        expert_in.reshape(D, 2 * PART).T, expert_out.reshape(PART, D),
    )


def solution(mesh):
    in_specs = (
        P("gx", "gy"),
        P(),
        P("gx", None),
        P("gx", None),
        P(None, "gx", "gy"),
        P("gy", "gx"),
        P(("gx", "gy"), None, None),
        P(("gx", "gy"), None, None),
    )
    return jax.shard_map(
        on_device, mesh=mesh, in_specs=in_specs, out_specs=P("gx", "gy"), check_vma=False
    )
```
